256 devices in a mesh: src: 16 (over y_lo, x, core), rec: 16 (over y_hi, z).
Axes of the slice: x: 4, y: 4 (y_hi: 2, y_lo: 2; y = y_hi * 2 + y_lo), z: 8, core: 2. Of those that a mesh axis runs over, the one named last changes fastest.
Arguments:
- kernel: bfloat16 [2, 32, 4096, 4096], P(None, None, 'src', 'rec'), may hold values from -0.09375 to 0.09375
- focusing: float32 [64, 4096, 128], P(None, ('rec', 'src')), may hold values from -6 to 6
- first_arrival: float32 [64, 4096, 128], P(None, ('rec', 'src')), may hold values from -6 to 6
- onset: int32 [64, 4096], replicated, may hold values from 32 to 127
Outputs:
- upgoing: float32 [64, 4096, 128], P(None, ('src', 'rec'))
- downgoing: float32 [64, 4096, 128], P(None, ('rec', 'src'))
The draws below stay inside these ranges and needn't reach their ends.
All inputs are finite; a program needn't handle non-finite values.
Results may differ from the reference program's by a relative error of at most 0.0029.
Values may be sent and summed in bfloat16 or wider, within the bound.
No kernel may reach another device: no remote copies, remote signals or barrier semaphores. Data moves between devices by JAX's collectives and lax.ppermute only.
A program may use at most 128 MiB of HBM per device.

```python
import jax
import jax.numpy as jnp
from jax import lax

NS = 4096
FREQ = 32
NT = 128
FOCAL = 64


def place_ends(values, rng, low, largest):
    index_at = [jax.random.randint(jax.random.fold_in(rng, axis), (), 0, length) for axis, length in enumerate(values.shape)]
    longest = values.shape.index(max(values.shape))
    next_to = index_at[:longest] + [(index_at[longest] + 1) % values.shape[longest]] + index_at[longest + 1:]
    return values.at[tuple(index_at)].set(low).at[tuple(next_to)].set(largest)


def level_of(own_key, extent, cuts, low, largest):
    level, own = 1.0, jax.random.fold_in(own_key, 6)
    for position, blocks in cuts:
        heights = jnp.exp(jax.random.uniform(jax.random.fold_in(own, position), (blocks,), jnp.float32, low / len(cuts), largest / len(cuts)))
        level = level * jnp.repeat(heights, extent[position] // blocks).reshape([-1 if axis == position else 1 for axis in range(len(extent))])
    return level


def gaussian(key, extent, deviation, limit, split=(), held_as=jnp.bfloat16):
    gain = level_of(key, extent, split, -0.22, 0.18) if split else 1.0
    array = jax.random.normal(key, extent, jnp.float32) * deviation * gain
    return jnp.minimum(jnp.maximum(array, -limit), limit).astype(held_as)


def setup_inputs(seed: int = 0) -> dict:
    arg_keys = jax.random.split(jax.random.key(seed), 5)
    return {
        "kernel": gaussian(arg_keys[0], (2, FREQ, NS, NS), NS ** -0.5, 0.09375, ((2, 16), (3, 16))),
        "focusing": gaussian(arg_keys[1], (FOCAL, NS, NT), 1.0, 6.0, ((1, 256),), jnp.float32),
        "first_arrival": gaussian(arg_keys[2], (FOCAL, NS, NT), 1.0, 6.0, ((1, 256),), jnp.float32),
        "onset": place_ends(jax.random.randint(arg_keys[3], (FOCAL, NS), NT // 4, NT), jax.random.fold_in(arg_keys[3], 1), NT // 4, NT - 1).astype(jnp.int32),
    }


HIGH = lax.Precision.HIGHEST


def tables(count, samples, flipped):
    steps = jnp.arange(samples, dtype=jnp.int32)
    if flipped:
        steps = samples - 1 - steps
    waves = jnp.arange(count, dtype=jnp.int32) + 1
    turns = (waves[:, None] * steps[None, :]) % samples
    angle = turns.astype(jnp.float32) * (2.0 * jnp.pi / samples)
    return jnp.cos(angle), jnp.sin(angle)


def spectra(traces, cosine, sine):
    real_part = jnp.einsum("pnt,kt->kpn", traces, cosine, precision=HIGH)
    imag_part = -jnp.einsum("pnt,kt->kpn", traces, sine, precision=HIGH)
    return real_part, imag_part


def synth(real_part, imag_part, cosine, sine, samples):
    first = jnp.einsum("kpn,kt->pnt", real_part, cosine, precision=HIGH)
    second = jnp.einsum("kpn,kt->pnt", imag_part, sine, precision=HIGH)
    return (2.0 / samples) * (first - second)


def reference(kernel, focusing, first_arrival, onset):
    samples = focusing.shape[2]
    count = kernel.shape[1]
    cosine, sine = tables(count, samples, False)
    rcosine, rsine = tables(count, samples, True)
    spec_re, spectrum_imaginary = spectra(focusing, cosine, sine)
    spec_re = spec_re.astype(jnp.bfloat16)
    spectrum_imaginary = spectrum_imaginary.astype(jnp.bfloat16)

    def forward(items):
        kernel_real, kernel_imaginary, a_re, a_im = items
        out_re = jnp.dot(a_re, kernel_real.T, preferred_element_type=jnp.float32) - jnp.dot(a_im, kernel_imaginary.T, preferred_element_type=jnp.float32)
        output_imaginary = jnp.dot(a_re, kernel_imaginary.T, preferred_element_type=jnp.float32) + jnp.dot(a_im, kernel_real.T, preferred_element_type=jnp.float32)
        return out_re, output_imaginary

    conv_re, conv_im = lax.map(forward, (kernel[0], kernel[1], spec_re, spectrum_imaginary))
    times = jnp.arange(samples, dtype=jnp.int32)
    window = times[None, None, :] < onset[:, :, None]
    upgoing = jnp.where(window, synth(conv_re, conv_im, cosine, sine, samples), 0.0)
    up_re, up_im = spectra(upgoing, cosine, sine)
    up_re = up_re.astype(jnp.bfloat16)
    up_im = up_im.astype(jnp.bfloat16)

    def backward(items):
        kernel_real, kernel_imaginary, a_re, a_im = items
        out_re = jnp.dot(a_re, kernel_real, preferred_element_type=jnp.float32) + jnp.dot(a_im, kernel_imaginary, preferred_element_type=jnp.float32)
        output_imaginary = jnp.dot(a_im, kernel_real, preferred_element_type=jnp.float32) - jnp.dot(a_re, kernel_imaginary, preferred_element_type=jnp.float32)
        return out_re, output_imaginary

    corr_re, corr_im = lax.map(backward, (kernel[0], kernel[1], up_re, up_im))
    reversed_part = synth(corr_re, corr_im, rcosine, rsine, samples)
    downgoing = first_arrival - jnp.where(window, reversed_part, 0.0)
    return upgoing, downgoing
```

```python
import functools

import numpy as np
import jax
import jax.numpy as jnp
from jax import lax
from jax.experimental import pallas as pl
from jax.experimental.pallas import tpu as pltpu
from jax.sharding import Mesh, PartitionSpec as P

HIGH = lax.Precision.HIGHEST
F32 = jnp.float32
BF16 = jnp.bfloat16
SPLITS = 1
KB = 4


def tables(count, samples, flipped):
    steps = np.arange(samples)
    if flipped:
        steps = samples - 1 - steps
    waves = np.arange(count) + 1
    angle = (waves[:, None] * steps[None, :] % samples) * (2.0 * np.pi / samples)
    return np.cos(angle).astype(np.float32), np.sin(angle).astype(np.float32)


def spectra(traces, cosine, sine):
    real_part = jnp.einsum("pnt,kt->knp", traces, cosine, precision=HIGH)
    imag_part = jnp.einsum("pnt,kt->knp", traces, -sine, precision=HIGH)
    return jnp.concatenate([real_part, imag_part], axis=2).astype(BF16)


def synth(packed, cosine, sine, samples):
    half = packed.shape[2] // 2
    first = jnp.einsum("knp,kt->pnt", packed[:, :, :half], cosine, precision=HIGH)
    second = jnp.einsum("knp,kt->pnt", packed[:, :, half:], sine, precision=HIGH)
    return 2.0 / samples * (first - second)


def onset_masked(onset, start, width, samples):
    limits = lax.dynamic_slice_in_dim(onset, start, width, 1)
    times = jnp.arange(samples, dtype=jnp.int32)
    return times[None, None, :] < limits[:, :, None]


def move(value, axis, step):
    size = lax.axis_size(axis)
    return lax.ppermute(value, axis, [(i, (i + step) % size) for i in range(size)])


def cross(direct, turned, sign):
    half = turned.shape[1] // 2
    lane = lax.broadcasted_iota(jnp.int32, turned.shape, 1)
    swapped = pltpu.roll(turned, half, 1)
    return direct + jnp.where(lane < half, -sign * swapped, sign * swapped)


def conv_body(where, kernel, *refs, pieces, order):
    ins, outs, spec = refs[:pieces], refs[pieces:-1], refs[-1]
    width, lanes = ins[0].shape[1:]
    count = len(order)
    z = where[1]
    for kk in range(kernel.shape[1]):
        for j in range(pieces):
            spec[kk, where[2 + j]] = ins[j][kk]
        rhs = spec[kk].reshape(pieces * width, lanes)
        parts = []
        for c in range(2):
            rows = [
                kernel[c, kk, pl.ds(pl.multiple_of(((z + d) % count) * width, width), width), :]
                for d in order
            ]
            parts.append(jnp.dot(jnp.concatenate(rows, axis=0), rhs, preferred_element_type=F32))
        out = cross(parts[0], parts[1], 1.0)
        for j in range(count):
            outs[j][kk] = out[j * width : (j + 1) * width].astype(outs[j].dtype)


def conv(where, kernel, pieces, order, starts, group, per):
    width, lanes = pieces[0].shape[1:]
    count = len(order)
    block = pl.BlockSpec((KB, width, lanes), lambda i, w: (i, 0, 0))
    base = group * (per // KB)
    return pl.pallas_call(
        functools.partial(conv_body, pieces=len(pieces), order=order),
        grid_spec=pltpu.PrefetchScalarGridSpec(
            num_scalar_prefetch=1,
            grid=(per // KB,),
            in_specs=[
                pl.BlockSpec(
                    (2, KB, count * width, kernel.shape[3]), lambda i, w: (0, base + i, w[0], 0)
                )
            ]
            + [block] * len(pieces),
            out_specs=[block] * count,
            scratch_shapes=[pltpu.VMEM((KB, len(pieces), width, lanes), BF16)],
        ),
        out_shape=[
            jax.ShapeDtypeStruct((per, width, lanes), BF16 if j < starts else F32)
            for j in range(count)
        ],
        name="conv",
    )(where, kernel, *pieces)


def corr_body(where, kernel, *refs, pieces):
    ins = refs[:pieces]
    away, stay = refs[pieces], refs[pieces + 1 : -2]
    spec, total = refs[-2:]
    width, lanes = ins[0].shape[1:]
    dims = (((0,), (0,)), ((), ()))
    for kk in range(kernel.shape[1]):
        for j in range(pieces):
            spec[kk, where[j]] = ins[j][kk]
        rhs = spec[kk].reshape(pieces * width, lanes)
        parts = [
            lax.dot_general(kernel[c, kk], rhs, dims, preferred_element_type=F32) for c in range(2)
        ]
        total[kk] = cross(parts[0], parts[1], -1.0).reshape(-1, width, lanes)
        for j in range(len(stay)):
            stay[j][kk] = total[kk, where[pieces + j]]
            away[j, kk] = total[kk, where[pieces + len(stay) + j]].astype(BF16)


def corr(where, kernel, pieces, group, per):
    width, lanes = pieces[0].shape[1:]
    rows, cols = kernel.shape[2:]
    half = cols // width // 2
    block = pl.BlockSpec((KB, width, lanes), lambda i, w: (i, 0, 0))
    base = group * (per // KB)
    out = pl.pallas_call(
        functools.partial(corr_body, pieces=len(pieces)),
        grid_spec=pltpu.PrefetchScalarGridSpec(
            num_scalar_prefetch=1,
            grid=(per // KB,),
            in_specs=[pl.BlockSpec((2, KB, rows, cols), lambda i, w: (0, base + i, 0, 0))]
            + [block] * len(pieces),
            out_specs=[pl.BlockSpec((half, KB, width, lanes), lambda i, w: (0, i, 0, 0))]
            + [block] * half,
            scratch_shapes=[
                pltpu.VMEM((KB, len(pieces), width, lanes), BF16),
                pltpu.VMEM((KB, 2 * half, width, lanes), F32),
            ],
        ),
        out_shape=[jax.ShapeDtypeStruct((half, per, width, lanes), BF16)]
        + [jax.ShapeDtypeStruct((per, width, lanes), F32)] * half,
        name="corr",
    )(where, kernel, *pieces)
    return out[0], out[1:]


def travel(starts, rest, axis, step):
    value = move(starts, axis, step)
    for share in rest:
        value = move((value.astype(F32) + share).astype(BF16), axis, step)
    return value.astype(F32)


def per_device(kernel, focusing, first_arrival, onset):
    points, width, samples = focusing.shape
    count = kernel.shape[1]
    per = count // SPLITS
    yl, x, c, yh, z = (lax.axis_index(name) for name in ("yl", "x", "c", "yh", "z"))
    nx, nz = lax.axis_size("x"), lax.axis_size("z")
    n_src, n_rec = 2 * nx * 2, 2 * nz
    src = (yl * nx + x) * 2 + c
    rec = yh * nz + z
    cosine, sine = tables(count, samples, False)
    rcosine, rsine = tables(count, samples, True)

    def src_at(dyl, dx, dc):
        return ((yl + dyl) % 2 * nx + (x + dx) % nx) * 2 + (c + dc) % 2

    def rec_at(dyh, dz):
        return (yh + dyh) % 2 * nz + (z + dz) % nz

    mask_up = onset_masked(onset, (src * n_rec + rec) * width, width, samples)
    mask_down = onset_masked(onset, (rec * n_src + src) * width, width, samples)

    own = spectra(focusing, cosine, sine)
    orders = [(4, 5, 3, 2, 1, 6, 7, 0), (4, 3, 5, 6, 7, 2, 1, 0)]
    shares = []
    for g in range(SPLITS):
        mine = own[g * per : (g + 1) * per]
        near = {(0, 0): mine, (1, 0): move(mine, "yl", 1)}
        near[0, -1] = move(mine, "x", 1)
        near[0, 1] = move(mine, "x", -1)
        near[0, 2] = move(near[0, -1], "x", 1)
        near[1, -1] = move(near[1, 0], "x", 1)
        near[1, 1] = move(near[1, 0], "x", -1)
        near[1, 2] = move(near[1, 1], "x", -1)
        keys = list(near)
        pieces = [near[key] for key in keys] + [move(near[key], "c", 1) for key in keys]
        spots = [src_at(a, b, d) for d in range(2) for a, b in keys]
        sums = []
        for s in range(2):
            where = jnp.stack([(yh + 1 - s) % 2, z] + spots).astype(jnp.int32)
            outs = conv(where, kernel, pieces, orders[s], 2, g, per)
            step = 1 - 2 * s
            far = travel(outs[0], outs[2:5], "z", step)
            back = travel(outs[1], outs[5:7], "z", -step)
            sums.append(far + back + outs[7])
        shares.append(move(sums[0], "yh", 1) + sums[1])
    share = jnp.concatenate(shares, axis=0)
    upgoing = jnp.where(mask_up, synth(share, cosine, sine, samples), 0.0)
    mine_up = spectra(upgoing, cosine, sine)

    totals = []
    for g in range(SPLITS):
        mine = mine_up[g * per : (g + 1) * per]
        found = {(0, 0): mine, (1, 0): move(mine, "yh", 1)}
        for s in range(2):
            step = 1 - 2 * s
            for direction, hops in ((step, nz // 2), (-step, nz // 2 - 1)):
                value = found[s, 0]
                for hop in range(1, hops + 1):
                    value = move(value, "z", direction)
                    found[s, -direction * hop] = value
        keys = list(found)
        spots = [rec_at(a, b) for a, b in keys]
        dests = [src_at(a, b, d) for d in range(2) for a in range(2) for b in range(nx)]
        where = jnp.stack(spots + dests).astype(jnp.int32)
        away, stay = corr(where, kernel, [found[key] for key in keys], g, per)
        taken = move(away, "c", 1)
        held = [[stay[a * nx + b] + taken[a * nx + b].astype(F32) for b in range(nx)] for a in range(2)]
        sums = []
        for s in range(2):
            row = held[1 - s]
            step = 1 - 2 * s
            far = travel(row[2].astype(BF16), [row[step % nx]], "x", step)
            back = travel(row[-step % nx].astype(BF16), [], "x", -step)
            sums.append(far + back + row[0])
        totals.append(move(sums[0], "yl", 1) + sums[1])
    total = jnp.concatenate(totals, axis=0)
    reversed_part = synth(total, rcosine, rsine, samples)
    downgoing = first_arrival - jnp.where(mask_down, reversed_part, 0.0)
    return upgoing, downgoing


def solution(mesh):
    fine = Mesh(mesh.devices.reshape(2, 4, 2, 2, 8), ("yl", "x", "c", "yh", "z"))
    src, rec = ("yl", "x", "c"), ("yh", "z")
    in_specs = (P(None, None, src, rec), P(None, rec + src, None), P(None, rec + src, None), P())
    out_specs = (P(None, src + rec, None), P(None, rec + src, None))
    return jax.shard_map(
        per_device, mesh=fine, in_specs=in_specs, out_specs=out_specs, check_vma=False
    )
```

```python
import functools

import numpy as np
import jax
import jax.numpy as jnp
from jax import lax
from jax.experimental import pallas as pl
from jax.experimental.pallas import tpu as pltpu
from jax.sharding import Mesh, PartitionSpec as P

HIGH = lax.Precision.HIGHEST
F32 = jnp.float32
BF16 = jnp.bfloat16
UNROLL = 8
NX, NZ = 4, 8
PAIRS = [(a, b) for a in range(2) for b in range(NX)]


def table(count, samples, flipped):
    steps = np.arange(samples)
    if flipped:
        steps = samples - 1 - steps
    waves = np.arange(count) + 1
    angle = (waves[:, None] * steps[None, :] % samples) * (2.0 * np.pi / samples)
    return np.concatenate([np.cos(angle), -np.sin(angle)]).astype(np.float32)


def local(body, outs, args, name, scratch=(), limit=4):
    vmem = pl.BlockSpec(memory_space=pltpu.VMEM)
    return pl.pallas_call(
        body,
        in_specs=[vmem] * len(args),
        out_specs=[vmem] * len(outs),
        out_shape=[pltpu.VMEM(shape, dtype) for shape, dtype in outs],
        scratch_shapes=list(scratch),
        compiler_params=pltpu.CompilerParams(vmem_limit_bytes=limit << 20),
        name=name,
    )(*[pltpu.with_memory_space_constraint(arg, pltpu.VMEM) for arg in args])


def src_at(dyl, dx, dc):
    yl, x, c = lax.axis_index("yl"), lax.axis_index("x"), lax.axis_index("c")
    return ((yl + dyl) & 1) * (2 * NX) + ((x + dx) & (NX - 1)) * 2 + ((c + dc) & 1)


def rec_at(dyh, dz):
    yh, z = lax.axis_index("yh"), lax.axis_index("z")
    return ((yh + dyh) & 1) * NZ + ((z + dz) & (NZ - 1))


def to_spec(forward, trace):
    dims = (((1,), (1,)), ((), ()))
    both = lax.dot_general(forward, trace, dims, precision=HIGH, preferred_element_type=F32)
    half = both.shape[0] // 2
    return jnp.concatenate([both[:half], both[half:]], axis=1)


def from_spec(packed, inverse):
    half = packed.shape[1] // 2
    stacked = jnp.concatenate([packed[:, :half], packed[:, half:]], axis=0)
    dims = (((0,), (0,)), ((), ()))
    return lax.dot_general(stacked, inverse, dims, precision=HIGH, preferred_element_type=F32)


def spectra_body(forward, traces, out, buf):
    for n in range(traces.shape[1]):
        buf[:, n, :] = to_spec(forward[...], traces[:, n, :])
    out[...] = buf[...].astype(BF16)


def middle_body(forward, inverse, onset, kept, taken, upgoing, out, total, buf):
    total[...] = kept[...] + taken[...]
    points, width, samples = upgoing.shape
    time = lax.broadcasted_iota(jnp.int32, (points, samples), 1)
    for n in range(width):
        trace = from_spec(total[:, n, :], inverse[...])
        trace = jnp.where(time < onset[:, n : n + 1], trace, 0.0)
        upgoing[:, n, :] = trace
        buf[:, n, :] = to_spec(forward[...], trace)
    out[...] = buf[...].astype(BF16)


def last_body(inverse, onset, first, kept, taken, downgoing, total):
    total[...] = kept[...] + taken[...].astype(F32)
    points, width, samples = downgoing.shape
    time = lax.broadcasted_iota(jnp.int32, (points, samples), 1)
    for n in range(width):
        trace = from_spec(total[:, n, :], inverse[...])
        trace = jnp.where(time < onset[:, n : n + 1], trace, 0.0)
        downgoing[:, n, :] = first[:, n, :] - trace


def cross(direct, turned, sign):
    half = turned.shape[1] // 2
    lane = lax.broadcasted_iota(jnp.int32, turned.shape, 1)
    swapped = pltpu.roll(turned, half, 1)
    return direct + jnp.where(lane < half, -sign * swapped, sign * swapped)


def steps(count, one):
    def step(i, carry):
        for u in range(UNROLL):
            one(i * UNROLL + u, u)
        return carry

    lax.fori_loop(0, count // UNROLL, step, 0)


def conv_body(kernel, *refs, spots):
    pieces = len(spots)
    ins, spec = refs[:pieces], refs[-1]
    lead_a, lead_b, p3, m5, p2, m6, p1, m7, home = refs[pieces:-1]
    width, lanes = ins[0].shape[1:]
    for j in range(pieces):
        spec[:, src_at(*spots[j])] = ins[j][...]
    order = [(s, dz) for s in range(2) for dz in range(NZ)]
    firsts = [pl.multiple_of(rec_at(1 - s, dz) * width, width) for s, dz in order]
    slots = {0: home, 1: p1, 2: p2, 3: p3, 5: m5, 6: m6, 7: m7}
    size = len(order) * width

    def one(kk, u):
        rhs = spec[kk].reshape(pieces * width, lanes)
        rows = [kernel[c, kk, pl.ds(first, width), :] for c in range(2) for first in firsts]
        both = jnp.dot(jnp.concatenate(rows, axis=0), rhs, preferred_element_type=F32)
        out = cross(both[:size], both[size:], 1.0)
        for j, (s, dz) in enumerate(order):
            part = out[j * width : (j + 1) * width]
            if dz == NZ // 2:
                (lead_a, lead_b)[s][kk] = part.astype(BF16)
            else:
                slots[dz][s, kk] = part

    steps(kernel.shape[1], one)


def corr_body(kernel, *refs, spots):
    pieces = len(spots)
    ins, (away, stay, spec, total) = refs[:pieces], refs[pieces:]
    width, lanes = ins[0].shape[1:]
    for j in range(pieces):
        spec[:, rec_at(*spots[j])] = ins[j][...]
    near = [src_at(a, b, 0) for a, b in PAIRS]
    far = [src_at(a, b, 1) for a, b in PAIRS]

    def one(kk, u):
        turned = spec[kk].reshape(pieces * width, lanes).T
        real, imag = [jnp.dot(turned, kernel[c, kk], preferred_element_type=F32) for c in range(2)]
        half = lanes // 2
        out = jnp.concatenate([real[:half] + imag[half:], real[half:] - imag[:half]], axis=0).T
        total[u] = out.reshape(-1, width, lanes)
        for j in range(len(PAIRS)):
            stay[j, kk] = total[u, near[j]]
            away[j, kk] = total[u, far[j]].astype(BF16)

    steps(kernel.shape[1], one)


def turn_body(plus, minus, share_p, share_m, out_p, out_m):
    out_p[0] = (plus[...].astype(F32) + share_p[0]).astype(BF16)
    out_p[1] = share_p[1].astype(BF16)
    out_m[0] = share_m[0].astype(BF16)
    out_m[1] = (minus[...].astype(F32) + share_m[1]).astype(BF16)


def pass_body(plus, minus, share_p, share_m, out_p, out_m):
    out_p[...] = (plus[...].astype(F32) + share_p[...]).astype(BF16)
    out_m[...] = (minus[...].astype(F32) + share_m[...]).astype(BF16)


def meet_body(plus, minus, home, send, keep):
    send[...] = plus[0].astype(F32) + minus[0].astype(F32) + home[0]
    keep[...] = plus[1].astype(F32) + minus[1].astype(F32) + home[1]


def held(stay, taken, s, b):
    j = PAIRS.index((1 - s, b))
    return stay[j] + taken[j].astype(F32)


def lead_x_body(stay, taken, out_p, out_m):
    out_p[...] = held(stay, taken, 0, 2).astype(BF16)
    out_m[...] = held(stay, taken, 1, 2).astype(BF16)


def turn_x_body(plus, minus, stay, taken, out_p, out_m):
    out_p[0] = (plus[...].astype(F32) + held(stay, taken, 0, 1)).astype(BF16)
    out_p[1] = held(stay, taken, 1, 1).astype(BF16)
    out_m[0] = held(stay, taken, 0, 3).astype(BF16)
    out_m[1] = (minus[...].astype(F32) + held(stay, taken, 1, 3)).astype(BF16)


def meet_x_body(plus, minus, stay, taken, send, keep):
    send[...] = (plus[0].astype(F32) + minus[0].astype(F32) + held(stay, taken, 0, 0)).astype(BF16)
    keep[...] = plus[1].astype(F32) + minus[1].astype(F32) + held(stay, taken, 1, 0)


def move(value, axis, step):
    size = lax.axis_size(axis)
    return lax.ppermute(value, axis, [(i, (i + step) % size) for i in range(size)])


def per_device(kernel, focusing, first_arrival, onset):
    points, width, samples = focusing.shape
    count = kernel.shape[1]
    lanes = 2 * points
    forward = jnp.asarray(table(count, samples, False))
    inverse = forward * (2.0 / samples)
    rinverse = jnp.asarray(table(count, samples, True)) * (2.0 / samples)
    src, rec = src_at(0, 0, 0), rec_at(0, 0)
    one, two = (count, width, lanes), (2, count, width, lanes)
    limits_up = lax.dynamic_slice_in_dim(onset, (src * 2 * NZ + rec) * width, width, 1)
    limits_down = lax.dynamic_slice_in_dim(onset, (rec * 4 * NX + src) * width, width, 1)
    buf = pltpu.VMEM(one, F32)

    (own,) = local(spectra_body, [(one, BF16)], [forward, focusing], "spectra", [buf])
    near = {(0, 0): own, (1, 0): move(own, "yl", 1)}
    near[0, -1] = move(own, "x", 1)
    near[0, 1] = move(own, "x", -1)
    near[0, 2] = move(near[0, -1], "x", 1)
    near[1, -1] = move(near[1, 0], "x", 1)
    near[1, 1] = move(near[1, 0], "x", -1)
    near[1, 2] = move(near[1, 1], "x", -1)
    pieces = list(near.values()) + [move(value, "c", 1) for value in near.values()]
    spots = [key + (d,) for d in range(2) for key in near]
    full = (len(spots), width, lanes)

    lead_a, lead_b, p3, m5, p2, m6, p1, m7, home = local(
        functools.partial(conv_body, spots=spots),
        [(one, BF16)] * 2 + [(two, F32)] * 7,
        [kernel] + pieces,
        "conv",
        [pltpu.VMEM((count,) + full, BF16)],
    )
    plus, minus = move(lead_a, "z", 1), move(lead_b, "z", -1)
    for body, share_p, share_m in ((turn_body, p3, m5), (pass_body, p2, m6), (pass_body, p1, m7)):
        plus, minus = local(body, [(two, BF16)] * 2, [plus, minus, share_p, share_m], "hop")
        plus, minus = move(plus, "z", 1), move(minus, "z", -1)
    send, keep = local(meet_body, [(one, F32)] * 2, [plus, minus, home], "meet")
    taken = move(send, "yh", 1)
    upgoing, mine = local(
        middle_body,
        [(focusing.shape, F32), (one, BF16)],
        [forward, inverse, limits_up, keep, taken],
        "middle",
        [buf, buf],
    )

    found = {(0, 0): mine, (1, 0): move(mine, "yh", 1)}
    for s in range(2):
        way = 1 - 2 * s
        for direction, hops in ((way, NZ // 2), (-way, NZ // 2 - 1)):
            value = found[s, 0]
            for hop in range(1, hops + 1):
                value = move(value, "z", direction)
                found[s, -direction * hop] = value
    away, stay = local(
        functools.partial(corr_body, spots=list(found)),
        [((len(PAIRS),) + one, BF16), ((len(PAIRS),) + one, F32)],
        [kernel] + list(found.values()),
        "corr",
        [pltpu.VMEM((count,) + full, BF16), pltpu.VMEM((UNROLL,) + full, F32)],
        8,
    )
    taken = move(away, "c", 1)
    plus, minus = local(lead_x_body, [(one, BF16)] * 2, [stay, taken], "lead_x")
    plus, minus = move(plus, "x", 1), move(minus, "x", -1)
    plus, minus = local(turn_x_body, [(two, BF16)] * 2, [plus, minus, stay, taken], "turn_x")
    plus, minus = move(plus, "x", 1), move(minus, "x", -1)
    send, keep = local(
        meet_x_body, [(one, BF16), (one, F32)], [plus, minus, stay, taken], "meet_x"
    )
    (downgoing,) = local(
        last_body,
        [(focusing.shape, F32)],
        [rinverse, limits_down, first_arrival, keep, move(send, "yl", 1)],
        "last",
        [buf],
    )
    return upgoing, downgoing


def solution(mesh):
    fine = Mesh(mesh.devices.reshape(2, NX, 2, 2, NZ), ("yl", "x", "c", "yh", "z"))
    src, rec = ("yl", "x", "c"), ("yh", "z")
    in_specs = (P(None, None, src, rec), P(None, rec + src, None), P(None, rec + src, None), P())
    out_specs = (P(None, src + rec, None), P(None, rec + src, None))
    return jax.shard_map(
        per_device, mesh=fine, in_specs=in_specs, out_specs=out_specs, check_vma=False
    )
```

```python
import functools

import numpy as np
import jax
import jax.numpy as jnp
from jax import lax
from jax.experimental import pallas as pl
from jax.experimental.pallas import tpu as pltpu
from jax.sharding import Mesh, PartitionSpec as P

HIGH = lax.Precision.HIGHEST
F32 = jnp.float32
BF16 = jnp.bfloat16
UNROLL = 8
NX, NZ = 4, 8
PAIRS = [(a, b) for a in range(2) for b in range(NX)]


def table(count, samples, flipped):
    steps = np.arange(samples)
    if flipped:
        steps = samples - 1 - steps
    waves = np.arange(count) + 1
    angle = (waves[:, None] * steps[None, :] % samples) * (2.0 * np.pi / samples)
    return np.concatenate([np.cos(angle), -np.sin(angle)]).astype(np.float32)


def local(body, outs, args, scratch=(), limit=4, source=None):
    vmem = pl.BlockSpec(memory_space=pltpu.VMEM)
    extra = [] if source is None else [source]
    return pl.pallas_call(
        body,
        in_specs=[pl.BlockSpec(memory_space=pl.ANY)] * len(extra) + [vmem] * len(args),
        out_specs=[vmem] * len(outs),
        out_shape=[pltpu.VMEM(shape, dtype) for shape, dtype in outs],
        scratch_shapes=list(scratch),
        compiler_params=pltpu.CompilerParams(vmem_limit_bytes=limit << 20),
    )(*extra, *[pltpu.with_memory_space_constraint(arg, pltpu.VMEM) for arg in args])


def src_at(dyl, dx, dc):
    yl, x, c = lax.axis_index("yl"), lax.axis_index("x"), lax.axis_index("c")
    return ((yl + dyl) & 1) * (2 * NX) + ((x + dx) & (NX - 1)) * 2 + ((c + dc) & 1)


def rec_at(dyh, dz):
    yh, z = lax.axis_index("yh"), lax.axis_index("z")
    return ((yh + dyh) & 1) * NZ + ((z + dz) & (NZ - 1))


def to_spec(forward, trace):
    dims = (((1,), (1,)), ((), ()))
    both = lax.dot_general(forward, trace, dims, precision=HIGH, preferred_element_type=F32)
    half = both.shape[0] // 2
    return jnp.concatenate([both[:half], both[half:]], axis=1)


def from_spec(packed, inverse):
    half = packed.shape[1] // 2
    stacked = jnp.concatenate([packed[:, :half], packed[:, half:]], axis=0)
    dims = (((0,), (0,)), ((), ()))
    return lax.dot_general(stacked, inverse, dims, precision=HIGH, preferred_element_type=F32)


def spectra_body(forward, traces, out, buf):
    for n in range(traces.shape[1]):
        buf[:, n, :] = to_spec(forward[...], traces[:, n, :])
    out[...] = buf[...].astype(BF16)


def middle_body(forward, inverse, onset, plus, minus, share, taken, upgoing, out, total, buf):
    total[...] = plus[...].astype(F32) + minus[...].astype(F32) + share[...] + taken[...]
    points, width, samples = upgoing.shape
    time = lax.broadcasted_iota(jnp.int32, (points, samples), 1)
    for n in range(width):
        trace = from_spec(total[:, n, :], inverse[...])
        trace = jnp.where(time < onset[:, n : n + 1], trace, 0.0)
        upgoing[:, n, :] = trace
        buf[:, n, :] = to_spec(forward[...], trace)
    out[...] = buf[...].astype(BF16)


def last_body(inverse, onset, first, kept, taken, downgoing, total):
    total[...] = kept[...] + taken[...].astype(F32)
    points, width, samples = downgoing.shape
    time = lax.broadcasted_iota(jnp.int32, (points, samples), 1)
    for n in range(width):
        trace = from_spec(total[:, n, :], inverse[...])
        trace = jnp.where(time < onset[:, n : n + 1], trace, 0.0)
        downgoing[:, n, :] = first[:, n, :] - trace


def cross(direct, turned, sign):
    half = turned.shape[1] // 2
    lane = lax.broadcasted_iota(jnp.int32, turned.shape, 1)
    swapped = pltpu.roll(turned, half, 1)
    return direct + jnp.where(lane < half, -sign * swapped, sign * swapped)


def stream(kernel, held_kernel, arrived, prepare, one):
    groups = kernel.shape[1] // UNROLL

    def fetch(i):
        part = pl.ds(i * UNROLL, UNROLL)
        return pltpu.make_async_copy(kernel.at[:, part], held_kernel.at[:, part], arrived.at[i])

    for i in range(groups):
        fetch(i).start()
    prepare()

    def step(i, carry):
        fetch(i).wait()
        for u in range(UNROLL):
            one(i * UNROLL + u, u)
        return carry

    lax.fori_loop(0, groups, step, 0)


def conv_body(source, *refs, spots):
    pieces = len(spots)
    ins, outs, (spec, kernel, arrived) = refs[:pieces], refs[pieces:-3], refs[-3:]
    width, lanes = ins[0].shape[1:]
    order = [(s, dz) for s in range(2) for dz in range(NZ)]
    firsts = [pl.multiple_of(rec_at(1 - s, dz) * width, width) for s, dz in order]
    size = len(order) * width

    def prepare():
        for j in range(pieces):
            spec[:, src_at(*spots[j])] = ins[j][...]

    def one(kk, u):
        rhs = spec[kk].reshape(pieces * width, lanes)
        rows = [kernel[c, kk, pl.ds(first, width), :] for c in range(2) for first in firsts]
        both = jnp.dot(jnp.concatenate(rows, axis=0), rhs, preferred_element_type=F32)
        out = cross(both[:size], both[size:], 1.0)
        for j in range(len(order)):
            outs[j][kk] = out[j * width : (j + 1) * width].astype(outs[j].dtype)

    stream(source, kernel, arrived, prepare, one)


def corr_body(source, *refs, spots):
    pieces = len(spots)
    ins, (away, stay, spec, total, kernel, arrived) = refs[:pieces], refs[pieces:]
    width, lanes = ins[0].shape[1:]
    near = [src_at(a, b, 0) for a, b in PAIRS]
    far = [src_at(a, b, 1) for a, b in PAIRS]

    def prepare():
        for j in range(pieces):
            spec[:, rec_at(*spots[j])] = ins[j][...]

    def one(kk, u):
        turned = spec[kk].reshape(pieces * width, lanes).T
        real, imag = [jnp.dot(turned, kernel[c, kk], preferred_element_type=F32) for c in range(2)]
        half = lanes // 2
        out = jnp.concatenate([real[:half] + imag[half:], real[half:] - imag[:half]], axis=0).T
        total[u] = out.reshape(-1, width, lanes)
        for j in range(len(PAIRS)):
            stay[j, kk] = total[u, near[j]]
            away[j, kk] = total[u, far[j]].astype(BF16)

    stream(source, kernel, arrived, prepare, one)


def hop_body(taken, share, out):
    out[...] = (taken[...].astype(F32) + share[...]).astype(BF16)


def meet_body(one_way, other_way, share, out):
    out[...] = one_way[...].astype(F32) + other_way[...].astype(F32) + share[...]


def held(stay, taken, s, b):
    j = PAIRS.index((1 - s, b))
    return stay[j] + taken[j].astype(F32)


def lead_x_body(stay, taken, out_p, out_m):
    out_p[...] = held(stay, taken, 0, 2).astype(BF16)
    out_m[...] = held(stay, taken, 1, 2).astype(BF16)


def turn_x_body(plus, minus, stay, taken, out_p, out_m):
    out_p[0] = (plus[...].astype(F32) + held(stay, taken, 0, 1)).astype(BF16)
    out_p[1] = held(stay, taken, 1, 1).astype(BF16)
    out_m[0] = held(stay, taken, 0, 3).astype(BF16)
    out_m[1] = (minus[...].astype(F32) + held(stay, taken, 1, 3)).astype(BF16)


def meet_x_body(plus, minus, stay, taken, send, keep):
    send[...] = (plus[0].astype(F32) + minus[0].astype(F32) + held(stay, taken, 0, 0)).astype(BF16)
    keep[...] = plus[1].astype(F32) + minus[1].astype(F32) + held(stay, taken, 1, 0)


def move(value, axis, step):
    size = lax.axis_size(axis)
    return lax.ppermute(value, axis, [(i, (i + step) % size) for i in range(size)])


def per_device(kernel, focusing, first_arrival, onset):
    points, width, samples = focusing.shape
    count = kernel.shape[1]
    lanes = 2 * points
    forward = jnp.asarray(table(count, samples, False))
    inverse = forward * (2.0 / samples)
    rinverse = jnp.asarray(table(count, samples, True)) * (2.0 / samples)
    src, rec = src_at(0, 0, 0), rec_at(0, 0)
    one, two = (count, width, lanes), (2, count, width, lanes)
    limits_up = lax.dynamic_slice_in_dim(onset, (src * 2 * NZ + rec) * width, width, 1)
    limits_down = lax.dynamic_slice_in_dim(onset, (rec * 4 * NX + src) * width, width, 1)
    buf = pltpu.VMEM(one, F32)
    bulk = [
        pltpu.VMEM(kernel.shape, BF16),
        pltpu.SemaphoreType.DMA((count // UNROLL,)),
    ]

    (own,) = local(spectra_body, [(one, BF16)], [forward, focusing], [buf])
    near = {(0, 0): own}
    near[0, -1] = move(own, "x", 1)
    near[0, 1] = move(own, "x", -1)
    near[1, 0] = move(own, "yl", 1)
    near[0, 2] = move(near[0, -1], "x", 1)
    near[1, 1] = move(near[1, 0], "x", -1)
    near[1, -1] = move(near[1, 0], "x", 1)
    near[1, 2] = move(near[1, 1], "x", -1)
    pieces = list(near.values()) + [move(value, "c", 1) for value in near.values()]
    spots = [key + (d,) for d in range(2) for key in near]
    full = (len(spots), width, lanes)

    leads = [(0, 4), (0, 5), (1, 3), (1, 4)]
    order = [(s, dz) for s in range(2) for dz in range(NZ)]
    outs = local(
        functools.partial(conv_body, spots=spots),
        [(one, BF16 if key in leads else F32) for key in order],
        pieces,
        [pltpu.VMEM((count,) + full, BF16)] + bulk,
        14,
        kernel,
    )
    share = dict(zip(order, outs))
    sums = {}
    for s in range(2):
        for sign, tag in ((1, "p"), (-1, "m")):
            hops = NZ // 2 - (tag == "mp"[s])
            value = share[s, sign * hops % NZ]
            for i in range(1, hops + 1):
                value = move(value, "z", sign)
                if i < hops:
                    left = share[s, sign * (hops - i) % NZ]
                    (value,) = local(hop_body, [(one, BF16)], [value, left])
            sums[s, tag] = value
    (send,) = local(meet_body, [(one, F32)], [sums[0, "p"], sums[0, "m"], share[0, 0]])
    taken = move(send, "yh", 1)
    upgoing, mine = local(
        middle_body,
        [(focusing.shape, F32), (one, BF16)],
        [forward, inverse, limits_up, sums[1, "p"], sums[1, "m"], share[1, 0], taken],
        [buf, buf],
    )

    found = {(0, 0): mine, (1, 0): move(mine, "yh", 1)}
    for s in range(2):
        for sign, tag in ((1, "p"), (-1, "m")):
            value = found[s, 0]
            for i in range(1, NZ // 2 + 1 - (tag == "mp"[s])):
                value = move(value, "z", sign)
                found[s, -sign * i] = value
    away, stay = local(
        functools.partial(corr_body, spots=list(found)),
        [((len(PAIRS),) + one, BF16), ((len(PAIRS),) + one, F32)],
        list(found.values()),
        [pltpu.VMEM((count,) + full, BF16), pltpu.VMEM((UNROLL,) + full, F32)] + bulk,
        18,
        kernel,
    )
    taken = move(away, "c", 1)
    plus, minus = local(lead_x_body, [(one, BF16)] * 2, [stay, taken])
    plus, minus = move(plus, "x", 1), move(minus, "x", -1)
    plus, minus = local(turn_x_body, [(two, BF16)] * 2, [plus, minus, stay, taken])
    plus, minus = move(plus, "x", 1), move(minus, "x", -1)
    send, keep = local(meet_x_body, [(one, BF16), (one, F32)], [plus, minus, stay, taken])
    (downgoing,) = local(
        last_body,
        [(focusing.shape, F32)],
        [rinverse, limits_down, first_arrival, keep, move(send, "yl", 1)],
        [buf],
    )
    return upgoing, downgoing


def solution(mesh):
    fine = Mesh(mesh.devices.reshape(2, NX, 2, 2, NZ), ("yl", "x", "c", "yh", "z"))
    src, rec = ("yl", "x", "c"), ("yh", "z")
    in_specs = (P(None, None, src, rec), P(None, rec + src, None), P(None, rec + src, None), P())
    out_specs = (P(None, src + rec, None), P(None, rec + src, None))

    return jax.shard_map(
        per_device, mesh=fine, in_specs=in_specs, out_specs=out_specs, check_vma=False
    )
```

```python
import functools

import numpy as np
import jax
import jax.numpy as jnp
from jax import lax
from jax.experimental import pallas as pl
from jax.experimental.pallas import tpu as pltpu
from jax.sharding import Mesh, PartitionSpec as P

HIGH = lax.Precision.HIGHEST
F32 = jnp.float32
BF16 = jnp.bfloat16
UNROLL = 8
NX, NZ = 4, 8
PAIRS = [(a, b) for a in range(2) for b in range(NX)]


def table(count, samples, flipped):
    steps = np.arange(samples)
    if flipped:
        steps = samples - 1 - steps
    waves = np.arange(count) + 1
    angle = (waves[:, None] * steps[None, :] % samples) * (2.0 * np.pi / samples)
    return np.concatenate([np.cos(angle), -np.sin(angle)]).astype(np.float32)


def local(body, outs, args, scratch=(), limit=4, source=None):
    vmem = pl.BlockSpec(memory_space=pltpu.VMEM)
    extra = []
    if source is not None:
        extra = [pltpu.with_memory_space_constraint(source, pltpu.HBM)]
    return pl.pallas_call(
        body,
        in_specs=[pl.BlockSpec(memory_space=pltpu.HBM)] * len(extra) + [vmem] * len(args),
        out_specs=[vmem] * len(outs),
        out_shape=[pltpu.VMEM(shape, dtype) for shape, dtype in outs],
        scratch_shapes=list(scratch),
        compiler_params=pltpu.CompilerParams(vmem_limit_bytes=limit << 20),
    )(*extra, *[pltpu.with_memory_space_constraint(arg, pltpu.VMEM) for arg in args])


def src_at(dyl, dx, dc):
    yl, x, c = lax.axis_index("yl"), lax.axis_index("x"), lax.axis_index("c")
    return ((yl + dyl) & 1) * (2 * NX) + ((x + dx) & (NX - 1)) * 2 + ((c + dc) & 1)


def rec_at(dyh, dz):
    yh, z = lax.axis_index("yh"), lax.axis_index("z")
    return ((yh + dyh) & 1) * NZ + ((z + dz) & (NZ - 1))


def to_spec(forward, trace):
    dims = (((1,), (1,)), ((), ()))
    both = lax.dot_general(forward, trace, dims, precision=HIGH, preferred_element_type=F32)
    half = both.shape[0] // 2
    return jnp.concatenate([both[:half], both[half:]], axis=1)


def from_spec(packed, inverse):
    half = packed.shape[1] // 2
    stacked = jnp.concatenate([packed[:, :half], packed[:, half:]], axis=0)
    dims = (((0,), (0,)), ((), ()))
    return lax.dot_general(stacked, inverse, dims, precision=HIGH, preferred_element_type=F32)


def spectra_body(forward, traces, out, buf):
    for n in range(traces.shape[1]):
        buf[:, n, :] = to_spec(forward[...], traces[:, n, :])
    out[...] = buf[...].astype(BF16)


def middle_body(forward, inverse, onset, plus, minus, share, taken, upgoing, out, total, buf):
    total[...] = plus[...].astype(F32) + minus[...].astype(F32) + share[...] + taken[...]
    points, width, samples = upgoing.shape
    time = lax.broadcasted_iota(jnp.int32, (points, samples), 1)
    for n in range(width):
        trace = from_spec(total[:, n, :], inverse[...])
        trace = jnp.where(time < onset[:, n : n + 1], trace, 0.0)
        upgoing[:, n, :] = trace
        buf[:, n, :] = to_spec(forward[...], trace)
    out[...] = buf[...].astype(BF16)


def last_body(inverse, onset, first, kept, taken, downgoing, total):
    total[...] = kept[...] + taken[...].astype(F32)
    points, width, samples = downgoing.shape
    time = lax.broadcasted_iota(jnp.int32, (points, samples), 1)
    for n in range(width):
        trace = from_spec(total[:, n, :], inverse[...])
        trace = jnp.where(time < onset[:, n : n + 1], trace, 0.0)
        downgoing[:, n, :] = first[:, n, :] - trace


def cross(direct, turned, sign):
    half = turned.shape[1] // 2
    lane = lax.broadcasted_iota(jnp.int32, turned.shape, 1)
    swapped = pltpu.roll(turned, half, 1)
    return direct + jnp.where(lane < half, -sign * swapped, sign * swapped)


def stream(kernel, held_kernel, arrived, prepare, one):
    groups = kernel.shape[1] // UNROLL

    def fetch(i):
        part = pl.ds(i * UNROLL, UNROLL)
        return pltpu.make_async_copy(kernel.at[:, part], held_kernel.at[:, part], arrived.at[i])

    for i in range(groups):
        fetch(i).start()
    prepare()

    def step(i, carry):
        fetch(i).wait()
        for u in range(UNROLL):
            one(i * UNROLL + u, u)
        return carry

    lax.fori_loop(0, groups, step, 0)


def pack_body(*refs):
    for i, ref in enumerate(refs[:-1]):
        refs[-1][i] = ref[...]


def pick_body(plus, minus, out_p, out_m):
    out_p[...] = plus[0]
    out_m[...] = minus[1]


def unpack(refs, spec, places):
    places = list(places)
    for ref in refs:
        if len(ref.shape) == 3:
            spec[:, places.pop(0)] = ref[...]
        else:
            for i in range(ref.shape[0]):
                spec[:, places.pop(0)] = ref[i]


def conv_body(source, *refs, spots, pieces):
    ins, outs, (spec, kernel, arrived) = refs[:pieces], refs[pieces:-3], refs[-3:]
    width, lanes = ins[0].shape[-2:]
    order = [(s, dz) for s in range(2) for dz in range(NZ)]
    firsts = [pl.multiple_of(rec_at(1 - s, dz) * width, width) for s, dz in order]
    size = len(order) * width

    def prepare():
        unpack(ins, spec, [src_at(*spot) for spot in spots])

    def one(kk, u):
        rhs = spec[kk].reshape(len(spots) * width, lanes)
        rows = [kernel[c, kk, pl.ds(first, width), :] for c in range(2) for first in firsts]
        both = jnp.dot(jnp.concatenate(rows, axis=0), rhs, preferred_element_type=F32)
        out = cross(both[:size], both[size:], 1.0)
        for j in range(len(order)):
            outs[j][kk] = out[j * width : (j + 1) * width].astype(outs[j].dtype)

    stream(source, kernel, arrived, prepare, one)


def corr_body(source, *refs, spots, pieces):
    ins, (away, stay, spec, total, kernel, arrived) = refs[:pieces], refs[pieces:]
    width, lanes = ins[0].shape[-2:]
    near = [src_at(a, b, 0) for a, b in PAIRS]
    far = [src_at(a, b, 1) for a, b in PAIRS]

    def prepare():
        unpack(ins, spec, [rec_at(*spot) for spot in spots])

    def one(kk, u):
        turned = spec[kk].reshape(len(spots) * width, lanes).T
        real, imag = [jnp.dot(turned, kernel[c, kk], preferred_element_type=F32) for c in range(2)]
        half = lanes // 2
        out = jnp.concatenate([real[:half] + imag[half:], real[half:] - imag[:half]], axis=0).T
        total[u] = out.reshape(-1, width, lanes)
        for j in range(len(PAIRS)):
            stay[j, kk] = total[u, near[j]]
            away[j, kk] = total[u, far[j]].astype(BF16)

    stream(source, kernel, arrived, prepare, one)


def hop_body(taken, share, out):
    out[...] = (taken[...].astype(F32) + share[...]).astype(BF16)


def meet_body(one_way, other_way, share, out):
    out[...] = one_way[...].astype(F32) + other_way[...].astype(F32) + share[...]


def held(stay, taken, s, b):
    j = PAIRS.index((1 - s, b))
    return stay[j] + taken[j].astype(F32)


def lead_x_body(stay, taken, out_p, out_m):
    out_p[...] = held(stay, taken, 0, 2).astype(BF16)
    out_m[...] = held(stay, taken, 1, 2).astype(BF16)


def turn_x_body(plus, minus, stay, taken, out_p, out_m):
    out_p[0] = (plus[...].astype(F32) + held(stay, taken, 0, 1)).astype(BF16)
    out_p[1] = held(stay, taken, 1, 1).astype(BF16)
    out_m[0] = held(stay, taken, 0, 3).astype(BF16)
    out_m[1] = (minus[...].astype(F32) + held(stay, taken, 1, 3)).astype(BF16)


def meet_x_body(plus, minus, stay, taken, send, keep):
    send[...] = (plus[0].astype(F32) + minus[0].astype(F32) + held(stay, taken, 0, 0)).astype(BF16)
    keep[...] = plus[1].astype(F32) + minus[1].astype(F32) + held(stay, taken, 1, 0)


def move(value, axis, step):
    size = lax.axis_size(axis)
    return lax.ppermute(value, axis, [(i, (i + step) % size) for i in range(size)])


def per_device(kernel, focusing, first_arrival, onset):
    points, width, samples = focusing.shape
    count = kernel.shape[1]
    lanes = 2 * points
    forward = jnp.asarray(table(count, samples, False))
    inverse = forward * (2.0 / samples)
    rinverse = jnp.asarray(table(count, samples, True)) * (2.0 / samples)
    src, rec = src_at(0, 0, 0), rec_at(0, 0)
    one, two = (count, width, lanes), (2, count, width, lanes)
    limits_up = lax.dynamic_slice_in_dim(onset, (src * 2 * NZ + rec) * width, width, 1)
    limits_down = lax.dynamic_slice_in_dim(onset, (rec * 4 * NX + src) * width, width, 1)
    buf = pltpu.VMEM(one, F32)
    bulk = [
        pltpu.VMEM(kernel.shape, BF16),
        pltpu.SemaphoreType.DMA((count // UNROLL,)),
    ]

    (own,) = local(spectra_body, [(one, BF16)], [forward, focusing], [buf])
    near = {(0, 0): own}
    near[0, -1] = move(own, "x", 1)
    near[0, 1] = move(own, "x", -1)
    near[1, 0] = move(own, "yl", 1)
    near[0, 2] = move(near[0, -1], "x", 1)
    near[1, 1] = move(near[1, 0], "x", -1)
    near[1, -1] = move(near[1, 0], "x", 1)
    near[1, 2] = move(near[1, 1], "x", -1)
    groups = [[(0, 0), (1, 0), (0, -1), (0, 1)], [(1, 1), (1, -1), (0, 2), (1, 2)]]
    pieces = list(near.values())
    spots = [key + (0,) for key in near] + [key + (1,) for group in groups for key in group]
    for group in groups:
        (packed,) = local(pack_body, [((len(group),) + one, BF16)], [near[key] for key in group])
        pieces.append(move(packed, "c", 1))
    full = (len(spots), width, lanes)

    leads = [(0, 4), (0, 5), (1, 3), (1, 4)]
    order = [(s, dz) for s in range(2) for dz in range(NZ)]
    outs = local(
        functools.partial(conv_body, spots=spots, pieces=len(pieces)),
        [(one, BF16 if key in leads else F32) for key in order],
        pieces,
        [pltpu.VMEM((count,) + full, BF16)] + bulk,
        14,
        kernel,
    )
    share = dict(zip(order, outs))
    sums = {}
    for s in range(2):
        for sign, tag in ((1, "p"), (-1, "m")):
            hops = NZ // 2 - (tag == "mp"[s])
            value = share[s, sign * hops % NZ]
            for i in range(1, hops + 1):
                value = move(value, "z", sign)
                if i < hops:
                    left = share[s, sign * (hops - i) % NZ]
                    (value,) = local(hop_body, [(one, BF16)], [value, left])
            sums[s, tag] = value
    (send,) = local(meet_body, [(one, F32)], [sums[0, "p"], sums[0, "m"], share[0, 0]])
    taken = move(send, "yh", 1)
    upgoing, mine = local(
        middle_body,
        [(focusing.shape, F32), (one, BF16)],
        [forward, inverse, limits_up, sums[1, "p"], sums[1, "m"], share[1, 0], taken],
        [buf, buf],
    )

    (pair,) = local(pack_body, [(two, BF16)], [mine, move(mine, "yh", 1)])
    plus = minus = pair
    pieces, spots = [pair], [(0, 0), (1, 0)]
    for i in range(1, NZ // 2):
        plus, minus = move(plus, "z", 1), move(minus, "z", -1)
        pieces += [plus, minus]
        spots += [(s, dz) for dz in (-i, i) for s in range(2)]
    plus, minus = local(pick_body, [(one, BF16)] * 2, [plus, minus])
    pieces += [move(plus, "z", 1), move(minus, "z", -1)]
    spots += [(s, NZ // 2) for s in range(2)]
    away, stay = local(
        functools.partial(corr_body, spots=spots, pieces=len(pieces)),
        [((len(PAIRS),) + one, BF16), ((len(PAIRS),) + one, F32)],
        pieces,
        [pltpu.VMEM((count,) + full, BF16), pltpu.VMEM((UNROLL,) + full, F32)] + bulk,
        18,
        kernel,
    )
    taken = move(away, "c", 1)
    plus, minus = local(lead_x_body, [(one, BF16)] * 2, [stay, taken])
    plus, minus = move(plus, "x", 1), move(minus, "x", -1)
    plus, minus = local(turn_x_body, [(two, BF16)] * 2, [plus, minus, stay, taken])
    plus, minus = move(plus, "x", 1), move(minus, "x", -1)
    send, keep = local(meet_x_body, [(one, BF16), (one, F32)], [plus, minus, stay, taken])
    (downgoing,) = local(
        last_body,
        [(focusing.shape, F32)],
        [rinverse, limits_down, first_arrival, keep, move(send, "yl", 1)],
        [buf],
    )
    return upgoing, downgoing


def solution(mesh):
    fine = Mesh(mesh.devices.reshape(2, NX, 2, 2, NZ), ("yl", "x", "c", "yh", "z"))
    src, rec = ("yl", "x", "c"), ("yh", "z")
    in_specs = (P(None, None, src, rec), P(None, rec + src, None), P(None, rec + src, None), P())
    out_specs = (P(None, src + rec, None), P(None, rec + src, None))

    return jax.shard_map(
        per_device, mesh=fine, in_specs=in_specs, out_specs=out_specs, check_vma=False
    )
```

```python
import functools

import numpy as np
import jax
import jax.numpy as jnp
from jax import lax
from jax.experimental import pallas as pl
from jax.experimental.pallas import tpu as pltpu
from jax.sharding import Mesh, PartitionSpec as P

HIGH = lax.Precision.HIGHEST
F32 = jnp.float32
BF16 = jnp.bfloat16
UNROLL = 8
NX, NZ = 4, 8
PAIRS = [(a, b) for a in range(2) for b in range(NX)]


def table(count, samples, flipped):
    steps = np.arange(samples)
    if flipped:
        steps = samples - 1 - steps
    waves = np.arange(count) + 1
    angle = (waves[:, None] * steps[None, :] % samples) * (2.0 * np.pi / samples)
    return np.concatenate([np.cos(angle), -np.sin(angle)]).astype(np.float32)


def local(body, outs, args, scratch=(), limit=4, source=None):
    vmem = pl.BlockSpec(memory_space=pltpu.VMEM)
    extra = []
    if source is not None:
        extra = [pltpu.with_memory_space_constraint(source, pltpu.HBM)]
    return pl.pallas_call(
        body,
        in_specs=[pl.BlockSpec(memory_space=pltpu.HBM)] * len(extra) + [vmem] * len(args),
        out_specs=[vmem] * len(outs),
        out_shape=[pltpu.VMEM(shape, dtype) for shape, dtype in outs],
        scratch_shapes=list(scratch),
        compiler_params=pltpu.CompilerParams(vmem_limit_bytes=limit << 20),
    )(*extra, *[pltpu.with_memory_space_constraint(arg, pltpu.VMEM) for arg in args])


def src_at(dyl, dx, dc):
    yl, x, c = lax.axis_index("yl"), lax.axis_index("x"), lax.axis_index("c")
    return ((yl + dyl) & 1) * (2 * NX) + ((x + dx) & (NX - 1)) * 2 + ((c + dc) & 1)


def rec_at(dyh, dz):
    yh, z = lax.axis_index("yh"), lax.axis_index("z")
    return ((yh + dyh) & 1) * NZ + ((z + dz) & (NZ - 1))


def to_spec(forward, trace):
    dims = (((1,), (1,)), ((), ()))
    both = lax.dot_general(forward, trace, dims, precision=HIGH, preferred_element_type=F32)
    half = both.shape[0] // 2
    return jnp.concatenate([both[:half], both[half:]], axis=1)


def from_spec(packed, inverse):
    half = packed.shape[1] // 2
    stacked = jnp.concatenate([packed[:, :half], packed[:, half:]], axis=0)
    dims = (((0,), (0,)), ((), ()))
    return lax.dot_general(stacked, inverse, dims, precision=HIGH, preferred_element_type=F32)


def spectra_body(forward, traces, out, buf):
    for n in range(traces.shape[1]):
        buf[:, n, :] = to_spec(forward[...], traces[:, n, :])
    out[...] = buf[...].astype(BF16)


def middle_body(forward, inverse, onset, plus, minus, share, far, upgoing, out, total, buf):
    ring = plus[...].astype(F32) + minus[...].astype(F32)
    total[...] = ring + (share[...] + far[0].astype(F32))
    points, width, samples = upgoing.shape
    time = lax.broadcasted_iota(jnp.int32, (points, samples), 1)
    for n in range(width):
        trace = from_spec(total[:, n, :], inverse[...])
        trace = jnp.where(time < onset[:, n : n + 1], trace, 0.0)
        upgoing[:, n, :] = trace
        buf[:, n, :] = to_spec(forward[...], trace)
    out[...] = buf[...].astype(BF16)


def last_body(inverse, onset, first, kept, taken, downgoing, total):
    total[...] = kept[...] + taken[...].astype(F32)
    points, width, samples = downgoing.shape
    time = lax.broadcasted_iota(jnp.int32, (points, samples), 1)
    for n in range(width):
        trace = from_spec(total[:, n, :], inverse[...])
        trace = jnp.where(time < onset[:, n : n + 1], trace, 0.0)
        downgoing[:, n, :] = first[:, n, :] - trace


def cross(direct, turned, sign):
    half = turned.shape[1] // 2
    lane = lax.broadcasted_iota(jnp.int32, turned.shape, 1)
    swapped = pltpu.roll(turned, half, 1)
    return direct + jnp.where(lane < half, -sign * swapped, sign * swapped)


def stream(kernel, held_kernel, arrived, row, prepare, one):
    groups = kernel.shape[1] // UNROLL
    rows = pl.ds(row, held_kernel.shape[2])

    def fetch(i):
        part = pl.ds(i * UNROLL, UNROLL)
        return pltpu.make_async_copy(
            kernel.at[:, part, rows], held_kernel.at[:, part], arrived.at[i]
        )

    for i in range(groups):
        fetch(i).start()
    prepare()

    def step(i, carry):
        fetch(i).wait()
        for u in range(UNROLL):
            one(i * UNROLL + u, u)
        return carry

    lax.fori_loop(0, groups, step, 0)


def pack_body(*refs):
    for i, ref in enumerate(refs[:-1]):
        refs[-1][i] = ref[...]


def unpack(refs, spec, places):
    places = list(places)
    for ref in refs:
        if len(ref.shape) == 3:
            spec[:, places.pop(0)] = ref[...]
        else:
            for i in range(ref.shape[0]):
                spec[:, places.pop(0)] = ref[i]


def conv_body(source, *refs, spots, pieces, dyh, slots):
    ins, outs, (spec, kernel, arrived) = refs[:pieces], refs[pieces:-3], refs[-3:]
    width, lanes = ins[0].shape[-2:]
    size = NZ * width
    z = lax.axis_index("z")
    firsts = [pl.multiple_of(((z + dz) & (NZ - 1)) * width, width) for dz in range(NZ)]
    row = pl.multiple_of(((lax.axis_index("yh") + dyh) & 1) * size, size)

    def prepare():
        unpack(ins, spec, [src_at(*spot) for spot in spots])

    def one(kk, u):
        rhs = spec[kk].reshape(len(spots) * width, lanes)
        rows = [kernel[c, kk, pl.ds(first, width), :] for c in range(2) for first in firsts]
        both = jnp.dot(jnp.concatenate(rows, axis=0), rhs, preferred_element_type=F32)
        out = cross(both[:size], both[size:], 1.0)
        for ref, slot in zip(outs, slots):
            for i, dz in enumerate(slot):
                part = out[dz * width : (dz + 1) * width].astype(ref.dtype)
                if len(slot) > 1:
                    ref[i, kk] = part
                else:
                    ref[kk] = part

    stream(source, kernel, arrived, row, prepare, one)


def corr_body(source, *refs, spots, pieces):
    ins, (away, stay, spec, total, kernel, arrived) = refs[:pieces], refs[pieces:]
    width, lanes = ins[0].shape[-2:]
    near = [src_at(a, b, 0) for a, b in PAIRS]
    far = [src_at(a, b, 1) for a, b in PAIRS]

    def prepare():
        unpack(ins, spec, [rec_at(*spot) for spot in spots])

    def one(kk, u):
        turned = spec[kk].reshape(len(spots) * width, lanes).T
        real, imag = [jnp.dot(turned, kernel[c, kk], preferred_element_type=F32) for c in range(2)]
        half = lanes // 2
        out = jnp.concatenate([real[:half] + imag[half:], real[half:] - imag[:half]], axis=0).T
        total[u] = out.reshape(-1, width, lanes)
        for j in range(len(PAIRS)):
            stay[j, kk] = total[u, near[j]]
            away[j, kk] = total[u, far[j]].astype(BF16)

    stream(source, kernel, arrived, 0, prepare, one)


def join_body(share, far, out):
    out[...] = (share[...] + far[...].astype(F32)).astype(BF16)


def hop_body(taken, share, far, out, *, at):
    out[...] = (taken[...].astype(F32) + share[...] + far[at].astype(F32)).astype(BF16)


def first_body(share, far, out, *, at):
    out[...] = (share[...] + far[at].astype(F32)).astype(BF16)


def held(stay, taken, s, b):
    j = PAIRS.index((1 - s, b))
    return stay[j] + taken[j].astype(F32)


def lead_x_body(stay, taken, out_p, out_m):
    out_p[...] = held(stay, taken, 0, 2).astype(BF16)
    out_m[...] = held(stay, taken, 1, 2).astype(BF16)


def turn_x_body(plus, minus, stay, taken, out_p, out_m):
    out_p[0] = (plus[...].astype(F32) + held(stay, taken, 0, 1)).astype(BF16)
    out_p[1] = held(stay, taken, 1, 1).astype(BF16)
    out_m[0] = held(stay, taken, 0, 3).astype(BF16)
    out_m[1] = (minus[...].astype(F32) + held(stay, taken, 1, 3)).astype(BF16)


def meet_x_body(plus, minus, stay, taken, send, keep):
    send[...] = (plus[0].astype(F32) + minus[0].astype(F32) + held(stay, taken, 0, 0)).astype(BF16)
    keep[...] = plus[1].astype(F32) + minus[1].astype(F32) + held(stay, taken, 1, 0)


def move(value, axis, step):
    size = lax.axis_size(axis)
    return lax.ppermute(value, axis, [(i, (i + step) % size) for i in range(size)])


def per_device(kernel, focusing, first_arrival, onset):
    points, width, samples = focusing.shape
    count = kernel.shape[1]
    lanes = 2 * points
    forward = jnp.asarray(table(count, samples, False))
    inverse = forward * (2.0 / samples)
    rinverse = jnp.asarray(table(count, samples, True)) * (2.0 / samples)
    src, rec = src_at(0, 0, 0), rec_at(0, 0)
    one, two = (count, width, lanes), (2, count, width, lanes)
    limits_up = lax.dynamic_slice_in_dim(onset, (src * 2 * NZ + rec) * width, width, 1)
    limits_down = lax.dynamic_slice_in_dim(onset, (rec * 4 * NX + src) * width, width, 1)
    buf = pltpu.VMEM(one, F32)
    arrived = pltpu.SemaphoreType.DMA((count // UNROLL,))
    half_kernel = (2, count, kernel.shape[2] // 2, kernel.shape[3])

    (own,) = local(spectra_body, [(one, BF16)], [forward, focusing], [buf])
    near = {(0, 0): own}
    near[0, -1] = move(own, "x", 1)
    near[0, 1] = move(own, "x", -1)
    near[1, 0] = move(own, "yl", 1)
    near[0, 2] = move(near[0, -1], "x", 1)
    near[1, 1] = move(near[1, 0], "x", -1)
    near[1, -1] = move(near[1, 0], "x", 1)
    near[1, 2] = move(near[1, 1], "x", -1)
    groups = [[(0, 0), (1, 0), (0, -1), (0, 1)], [(1, 1), (1, -1), (0, 2), (1, 2)]]
    pieces = list(near.values())
    spots = [key + (0,) for key in near] + [key + (1,) for group in groups for key in group]
    for group in groups:
        (packed,) = local(pack_body, [((len(group),) + one, BF16)], [near[key] for key in group])
        pieces.append(move(packed, "c", 1))
    full = (len(spots), width, lanes)

    def conv(dyh, slots, dtype):
        return local(
            functools.partial(
                conv_body, spots=spots, pieces=len(pieces), dyh=dyh, slots=slots
            ),
            [(((len(slot),) if len(slot) > 1 else ()) + one, dtype) for slot in slots],
            pieces,
            [pltpu.VMEM((count,) + full, BF16), pltpu.VMEM(half_kernel, BF16), arrived],
            9,
            kernel,
        )

    slots = [(4,), (3, 5), (2, 6), (0, 1, 7)]
    far = [move(value, "yh", 1) for value in conv(1, slots, BF16)]
    share = conv(0, [(dz,) for dz in range(NZ)], F32)
    (plus,) = local(join_body, [(one, BF16)], [share[4], far[0]])
    plus = move(plus, "z", 1)
    first = functools.partial(first_body, at=1)
    (minus,) = local(first, [(one, BF16)], [share[5], far[1]])
    minus = move(minus, "z", -1)
    for dz, group, at in ((3, 1, 0), (2, 2, 0), (1, 3, 1)):
        body = functools.partial(hop_body, at=at)
        (plus,) = local(body, [(one, BF16)], [plus, share[dz], far[group]])
        plus = move(plus, "z", 1)
    for dz, group, at in ((6, 2, 1), (7, 3, 2)):
        body = functools.partial(hop_body, at=at)
        (minus,) = local(body, [(one, BF16)], [minus, share[dz], far[group]])
        minus = move(minus, "z", -1)
    upgoing, mine = local(
        middle_body,
        [(focusing.shape, F32), (one, BF16)],
        [forward, inverse, limits_up, plus, minus, share[0], far[3]],
        [buf, buf],
    )

    pieces, spots = [mine, move(mine, "yh", 1)], [(0, 0), (1, 0)]
    plus = minus = mine
    for i in range(1, NZ // 2):
        plus, minus = move(plus, "z", 1), move(minus, "z", -1)
        (pair,) = local(pack_body, [(two, BF16)], [plus, minus])
        pieces += [plus, minus, move(pair, "yh", 1)]
        spots += [(s, dz) for s in range(2) for dz in (-i, i)]
    plus = move(plus, "z", 1)
    pieces += [plus, move(plus, "yh", 1)]
    spots += [(s, NZ // 2) for s in range(2)]
    away, stay = local(
        functools.partial(corr_body, spots=spots, pieces=len(pieces)),
        [((len(PAIRS),) + one, BF16), ((len(PAIRS),) + one, F32)],
        pieces,
        [pltpu.VMEM((count,) + full, BF16), pltpu.VMEM((UNROLL,) + full, F32)]
        + [pltpu.VMEM(kernel.shape, BF16), arrived],
        18,
        kernel,
    )
    taken = move(away, "c", 1)
    plus, minus = local(lead_x_body, [(one, BF16)] * 2, [stay, taken])
    plus, minus = move(plus, "x", 1), move(minus, "x", -1)
    plus, minus = local(turn_x_body, [(two, BF16)] * 2, [plus, minus, stay, taken])
    plus, minus = move(plus, "x", 1), move(minus, "x", -1)
    send, keep = local(meet_x_body, [(one, BF16), (one, F32)], [plus, minus, stay, taken])
    (downgoing,) = local(
        last_body,
        [(focusing.shape, F32)],
        [rinverse, limits_down, first_arrival, keep, move(send, "yl", 1)],
        [buf],
    )
    return upgoing, downgoing


def solution(mesh):
    fine = Mesh(mesh.devices.reshape(2, NX, 2, 2, NZ), ("yl", "x", "c", "yh", "z"))
    src, rec = ("yl", "x", "c"), ("yh", "z")
    in_specs = (P(None, None, src, rec), P(None, rec + src, None), P(None, rec + src, None), P())
    out_specs = (P(None, src + rec, None), P(None, rec + src, None))

    return jax.shard_map(
        per_device, mesh=fine, in_specs=in_specs, out_specs=out_specs, check_vma=False
    )
```

```python
import functools

import numpy as np
import jax
import jax.numpy as jnp
from jax import lax
from jax.experimental import pallas as pl
from jax.experimental.pallas import tpu as pltpu
from jax.sharding import Mesh, PartitionSpec as P

HIGH = lax.Precision.HIGHEST
F32 = jnp.float32
BF16 = jnp.bfloat16
UNROLL = 8
NX, NZ = 4, 8
PAIRS = [(a, b) for a in range(2) for b in range(NX)]


def table(count, samples, flipped):
    steps = np.arange(samples)
    if flipped:
        steps = samples - 1 - steps
    waves = np.arange(count) + 1
    angle = (waves[:, None] * steps[None, :] % samples) * (2.0 * np.pi / samples)
    return np.concatenate([np.cos(angle), -np.sin(angle)]).astype(np.float32)


def local(body, outs, args, scratch=(), limit=4, source=None):
    vmem = pl.BlockSpec(memory_space=pltpu.VMEM)
    extra = []
    if source is not None:
        extra = [pltpu.with_memory_space_constraint(source, pltpu.HBM)]
    return pl.pallas_call(
        body,
        in_specs=[pl.BlockSpec(memory_space=pltpu.HBM)] * len(extra) + [vmem] * len(args),
        out_specs=[vmem] * len(outs),
        out_shape=[pltpu.VMEM(shape, dtype) for shape, dtype in outs],
        scratch_shapes=list(scratch),
        compiler_params=pltpu.CompilerParams(vmem_limit_bytes=limit << 20),
    )(*extra, *[pltpu.with_memory_space_constraint(arg, pltpu.VMEM) for arg in args])


def src_at(dyl, dx, dc):
    yl, x, c = lax.axis_index("yl"), lax.axis_index("x"), lax.axis_index("c")
    return ((yl + dyl) & 1) * (2 * NX) + ((x + dx) & (NX - 1)) * 2 + ((c + dc) & 1)


def rec_at(dyh, dz):
    yh, z = lax.axis_index("yh"), lax.axis_index("z")
    return ((yh + dyh) & 1) * NZ + ((z + dz) & (NZ - 1))


def to_spec(forward, trace):
    dims = (((1,), (1,)), ((), ()))
    both = lax.dot_general(forward, trace, dims, precision=HIGH, preferred_element_type=F32)
    half = both.shape[0] // 2
    return jnp.concatenate([both[:half], both[half:]], axis=1)


def from_spec(packed, inverse):
    half = packed.shape[1] // 2
    stacked = jnp.concatenate([packed[:, :half], packed[:, half:]], axis=0)
    dims = (((0,), (0,)), ((), ()))
    return lax.dot_general(stacked, inverse, dims, precision=HIGH, preferred_element_type=F32)


def spectra_body(forward_hbm, traces_hbm, out, forward, traces, buf, arrived):
    width = traces.shape[1]
    half = width // 2
    fetches = [pltpu.make_async_copy(forward_hbm, forward, arrived.at[2])]
    for i in range(2):
        part = pl.ds(i * half, half)
        fetches.append(
            pltpu.make_async_copy(traces_hbm.at[:, part], traces.at[:, part], arrived.at[i])
        )
    for fetch in fetches:
        fetch.start()
    fetches[0].wait()
    for n in range(width):
        if n % half == 0:
            fetches[1 + n // half].wait()
        buf[:, n, :] = to_spec(forward[...], traces[:, n, :])
    out[...] = buf[...].astype(BF16)


def spectra(forward, traces):
    count, lanes = forward.shape[0] // 2, 2 * traces.shape[0]
    shape = (count, traces.shape[1], lanes)
    hbm = pltpu.HBM
    return pl.pallas_call(
        spectra_body,
        in_specs=[pl.BlockSpec(memory_space=hbm)] * 2,
        out_specs=pl.BlockSpec(memory_space=pltpu.VMEM),
        out_shape=pltpu.VMEM(shape, BF16),
        scratch_shapes=[
            pltpu.VMEM(forward.shape, F32),
            pltpu.VMEM(traces.shape, F32),
            pltpu.VMEM(shape, F32),
            pltpu.SemaphoreType.DMA((3,)),
        ],
        compiler_params=pltpu.CompilerParams(vmem_limit_bytes=4 << 20),
        name="spectra",
    )(*[pltpu.with_memory_space_constraint(arg, hbm) for arg in (forward, traces)])


def middle_body(forward, inverse, onset, plus, minus, share, far, upgoing, out, total, buf):
    ring = plus[...].astype(F32) + minus[...].astype(F32)
    total[...] = ring + (share[...] + far[...].astype(F32))
    points, width, samples = upgoing.shape
    time = lax.broadcasted_iota(jnp.int32, (points, samples), 1)
    for n in range(width):
        trace = from_spec(total[:, n, :], inverse[...])
        trace = jnp.where(time < onset[:, n : n + 1], trace, 0.0)
        upgoing[:, n, :] = trace
        buf[:, n, :] = to_spec(forward[...], trace)
    out[...] = buf[...].astype(BF16)


def last_body(inverse, onset, first, kept, taken, downgoing, total):
    total[...] = kept[...] + taken[...].astype(F32)
    points, width, samples = downgoing.shape
    time = lax.broadcasted_iota(jnp.int32, (points, samples), 1)
    for n in range(width):
        trace = from_spec(total[:, n, :], inverse[...])
        trace = jnp.where(time < onset[:, n : n + 1], trace, 0.0)
        downgoing[:, n, :] = first[:, n, :] - trace


def cross(direct, turned, sign):
    half = turned.shape[1] // 2
    lane = lax.broadcasted_iota(jnp.int32, turned.shape, 1)
    swapped = pltpu.roll(turned, half, 1)
    return direct + jnp.where(lane < half, -sign * swapped, sign * swapped)


def stream(kernel, held_kernel, arrived, row, prepare, one):
    groups = kernel.shape[1] // UNROLL
    rows = pl.ds(row, held_kernel.shape[2])

    def fetch(i):
        part = pl.ds(i * UNROLL, UNROLL)
        return pltpu.make_async_copy(
            kernel.at[:, part, rows], held_kernel.at[:, part], arrived.at[i]
        )

    for i in range(groups):
        fetch(i).start()
    prepare()

    def step(i, carry):
        fetch(i).wait()
        for u in range(UNROLL):
            one(i * UNROLL + u, u)
        return carry

    lax.fori_loop(0, groups, step, 0)


def pack_body(*refs):
    for i, ref in enumerate(refs[:-1]):
        refs[-1][i] = ref[...]


def unpack(refs, spec, places):
    places = list(places)
    for ref in refs:
        if len(ref.shape) == 3:
            spec[:, places.pop(0)] = ref[...]
        else:
            for i in range(ref.shape[0]):
                spec[:, places.pop(0)] = ref[i]


def conv_body(source, *refs, spots, pieces, dyh, slots):
    ins, outs, (spec, kernel, arrived) = refs[:pieces], refs[pieces:-3], refs[-3:]
    width, lanes = ins[0].shape[-2:]
    size = NZ * width
    z = lax.axis_index("z")
    firsts = [pl.multiple_of(((z + dz) & (NZ - 1)) * width, width) for dz in range(NZ)]
    row = pl.multiple_of(((lax.axis_index("yh") + dyh) & 1) * size, size)

    def prepare():
        unpack(ins, spec, [src_at(*spot) for spot in spots])

    def one(kk, u):
        rhs = spec[kk].reshape(len(spots) * width, lanes)
        rows = [kernel[c, kk, pl.ds(first, width), :] for c in range(2) for first in firsts]
        both = jnp.dot(jnp.concatenate(rows, axis=0), rhs, preferred_element_type=F32)
        out = cross(both[:size], both[size:], 1.0)
        for ref, slot in zip(outs, slots):
            for i, dz in enumerate(slot):
                part = out[dz * width : (dz + 1) * width].astype(ref.dtype)
                if len(slot) > 1:
                    ref[i, kk] = part
                else:
                    ref[kk] = part

    stream(source, kernel, arrived, row, prepare, one)


def corr_body(source, *refs, spots, pieces):
    ins, (away, stay, spec, total, kernel, arrived) = refs[:pieces], refs[pieces:]
    width, lanes = ins[0].shape[-2:]
    near = [src_at(a, b, 0) for a, b in PAIRS]
    far = [src_at(a, b, 1) for a, b in PAIRS]

    def prepare():
        unpack(ins, spec, [rec_at(*spot) for spot in spots])

    def one(kk, u):
        turned = spec[kk].reshape(len(spots) * width, lanes).T
        real, imag = [jnp.dot(turned, kernel[c, kk], preferred_element_type=F32) for c in range(2)]
        half = lanes // 2
        out = jnp.concatenate([real[:half] + imag[half:], real[half:] - imag[:half]], axis=0).T
        total[u] = out.reshape(-1, width, lanes)
        for j in range(len(PAIRS)):
            stay[j, kk] = total[u, near[j]]
            away[j, kk] = total[u, far[j]].astype(BF16)

    stream(source, kernel, arrived, 0, prepare, one)


def join_body(share, far, out):
    out[...] = (share[...] + far[...].astype(F32)).astype(BF16)


def hop_body(taken, share, far, out, *, at):
    out[...] = (taken[...].astype(F32) + share[...] + far[at].astype(F32)).astype(BF16)


def first_body(share, far, out, *, at):
    out[...] = (share[...] + far[at].astype(F32)).astype(BF16)


def held(stay, taken, s, b):
    j = PAIRS.index((1 - s, b))
    return stay[j] + taken[j].astype(F32)


def lead_x_body(stay, taken, out_p, out_m):
    out_p[...] = held(stay, taken, 0, 2).astype(BF16)
    out_m[...] = held(stay, taken, 1, 2).astype(BF16)


def turn_x_body(plus, minus, stay, taken, out_p, out_m):
    out_p[0] = (plus[...].astype(F32) + held(stay, taken, 0, 1)).astype(BF16)
    out_p[1] = held(stay, taken, 1, 1).astype(BF16)
    out_m[0] = held(stay, taken, 0, 3).astype(BF16)
    out_m[1] = (minus[...].astype(F32) + held(stay, taken, 1, 3)).astype(BF16)


def meet_x_body(plus, minus, stay, taken, send, keep):
    send[...] = (plus[0].astype(F32) + minus[0].astype(F32) + held(stay, taken, 0, 0)).astype(BF16)
    keep[...] = plus[1].astype(F32) + minus[1].astype(F32) + held(stay, taken, 1, 0)


def move(value, axis, step):
    size = lax.axis_size(axis)
    return lax.ppermute(value, axis, [(i, (i + step) % size) for i in range(size)])


def per_device(kernel, focusing, first_arrival, onset):
    points, width, samples = focusing.shape
    count = kernel.shape[1]
    lanes = 2 * points
    forward = jnp.asarray(table(count, samples, False))
    inverse = forward * (2.0 / samples)
    rinverse = jnp.asarray(table(count, samples, True)) * (2.0 / samples)
    src, rec = src_at(0, 0, 0), rec_at(0, 0)
    one, two = (count, width, lanes), (2, count, width, lanes)
    limits_up = lax.dynamic_slice_in_dim(onset, (src * 2 * NZ + rec) * width, width, 1)
    limits_down = lax.dynamic_slice_in_dim(onset, (rec * 4 * NX + src) * width, width, 1)
    buf = pltpu.VMEM(one, F32)
    arrived = pltpu.SemaphoreType.DMA((count // UNROLL,))
    half_kernel = (2, count, kernel.shape[2] // 2, kernel.shape[3])

    own = spectra(forward, focusing)
    near = {(0, 0): own}
    near[0, -1] = move(own, "x", 1)
    near[0, 1] = move(own, "x", -1)
    near[1, 0] = move(own, "yl", 1)
    near[0, 2] = move(near[0, -1], "x", 1)
    near[1, 1] = move(near[1, 0], "x", -1)
    near[1, -1] = move(near[1, 0], "x", 1)
    near[1, 2] = move(near[1, 1], "x", -1)
    groups = [[(0, 0), (1, 0), (0, -1), (0, 1)], [(1, 1), (1, -1), (0, 2), (1, 2)]]
    pieces = list(near.values())
    spots = [key + (0,) for key in near] + [key + (1,) for group in groups for key in group]
    for group in groups:
        (packed,) = local(pack_body, [((len(group),) + one, BF16)], [near[key] for key in group])
        pieces.append(move(packed, "c", 1))
    full = (len(spots), width, lanes)

    def conv(dyh, slots, dtype):
        return local(
            functools.partial(
                conv_body, spots=spots, pieces=len(pieces), dyh=dyh, slots=slots
            ),
            [(((len(slot),) if len(slot) > 1 else ()) + one, dtype) for slot in slots],
            pieces,
            [pltpu.VMEM((count,) + full, BF16), pltpu.VMEM(half_kernel, BF16), arrived],
            9,
            kernel,
        )

    slots = [(4,), (3, 5), (2, 6), (1, 7), (0,)]
    far = [move(value, "yh", 1) for value in conv(1, slots, BF16)]
    share = conv(0, [(dz,) for dz in range(NZ)], F32)
    (plus,) = local(join_body, [(one, BF16)], [share[4], far[0]])
    plus = move(plus, "z", 1)
    first = functools.partial(first_body, at=1)
    (minus,) = local(first, [(one, BF16)], [share[5], far[1]])
    minus = move(minus, "z", -1)
    for dz, group, at in ((3, 1, 0), (2, 2, 0), (1, 3, 0)):
        body = functools.partial(hop_body, at=at)
        (plus,) = local(body, [(one, BF16)], [plus, share[dz], far[group]])
        plus = move(plus, "z", 1)
    for dz, group, at in ((6, 2, 1), (7, 3, 1)):
        body = functools.partial(hop_body, at=at)
        (minus,) = local(body, [(one, BF16)], [minus, share[dz], far[group]])
        minus = move(minus, "z", -1)
    upgoing, mine = local(
        middle_body,
        [(focusing.shape, F32), (one, BF16)],
        [forward, inverse, limits_up, plus, minus, share[0], far[4]],
        [buf, buf],
    )

    pieces, spots = [mine, move(mine, "yh", 1)], [(0, 0), (1, 0)]
    plus = minus = mine
    for i in range(1, NZ // 2):
        plus, minus = move(plus, "z", 1), move(minus, "z", -1)
        (pair,) = local(pack_body, [(two, BF16)], [plus, minus])
        pieces += [plus, minus, move(pair, "yh", 1)]
        spots += [(s, dz) for s in range(2) for dz in (-i, i)]
    plus = move(plus, "z", 1)
    pieces += [plus, move(plus, "yh", 1)]
    spots += [(s, NZ // 2) for s in range(2)]
    away, stay = local(
        functools.partial(corr_body, spots=spots, pieces=len(pieces)),
        [((len(PAIRS),) + one, BF16), ((len(PAIRS),) + one, F32)],
        pieces,
        [pltpu.VMEM((count,) + full, BF16), pltpu.VMEM((UNROLL,) + full, F32)]
        + [pltpu.VMEM(kernel.shape, BF16), arrived],
        18,
        kernel,
    )
    taken = move(away, "c", 1)
    plus, minus = local(lead_x_body, [(one, BF16)] * 2, [stay, taken])
    plus, minus = move(plus, "x", 1), move(minus, "x", -1)
    plus, minus = local(turn_x_body, [(two, BF16)] * 2, [plus, minus, stay, taken])
    plus, minus = move(plus, "x", 1), move(minus, "x", -1)
    send, keep = local(meet_x_body, [(one, BF16), (one, F32)], [plus, minus, stay, taken])
    (downgoing,) = local(
        last_body,
        [(focusing.shape, F32)],
        [rinverse, limits_down, first_arrival, keep, move(send, "yl", 1)],
        [buf],
    )
    return upgoing, downgoing


def solution(mesh):
    fine = Mesh(mesh.devices.reshape(2, NX, 2, 2, NZ), ("yl", "x", "c", "yh", "z"))
    src, rec = ("yl", "x", "c"), ("yh", "z")
    in_specs = (P(None, None, src, rec), P(None, rec + src, None), P(None, rec + src, None), P())
    out_specs = (P(None, src + rec, None), P(None, rec + src, None))

    return jax.shard_map(
        per_device, mesh=fine, in_specs=in_specs, out_specs=out_specs, check_vma=False
    )
```

```python
import functools

import numpy as np
import jax
import jax.numpy as jnp
from jax import lax
from jax.experimental import pallas as pl
from jax.experimental.pallas import tpu as pltpu
from jax.sharding import Mesh, PartitionSpec as P

HIGH = lax.Precision.HIGHEST
F32 = jnp.float32
BF16 = jnp.bfloat16
UNROLL = 8
NX, NZ = 4, 8
PAIRS = [(a, b) for a in range(2) for b in range(NX)]


def table(count, samples, flipped):
    steps = np.arange(samples)
    if flipped:
        steps = samples - 1 - steps
    waves = np.arange(count) + 1
    angle = (waves[:, None] * steps[None, :] % samples) * (2.0 * np.pi / samples)
    return np.concatenate([np.cos(angle), -np.sin(angle)]).astype(np.float32)


def local(body, outs, args, scratch=(), limit=4, source=None):
    vmem = pl.BlockSpec(memory_space=pltpu.VMEM)
    extra = []
    if source is not None:
        extra = [pltpu.with_memory_space_constraint(source, pltpu.HBM)]
    return pl.pallas_call(
        body,
        in_specs=[pl.BlockSpec(memory_space=pltpu.HBM)] * len(extra) + [vmem] * len(args),
        out_specs=[vmem] * len(outs),
        out_shape=[pltpu.VMEM(shape, dtype) for shape, dtype in outs],
        scratch_shapes=list(scratch),
        compiler_params=pltpu.CompilerParams(vmem_limit_bytes=limit << 20),
    )(*extra, *[pltpu.with_memory_space_constraint(arg, pltpu.VMEM) for arg in args])


def src_at(dyl, dx, dc):
    yl, x, c = lax.axis_index("yl"), lax.axis_index("x"), lax.axis_index("c")
    return ((yl + dyl) & 1) * (2 * NX) + ((x + dx) & (NX - 1)) * 2 + ((c + dc) & 1)


def rec_at(dyh, dz):
    yh, z = lax.axis_index("yh"), lax.axis_index("z")
    return ((yh + dyh) & 1) * NZ + ((z + dz) & (NZ - 1))


def to_spec(forward, trace):
    dims = (((1,), (1,)), ((), ()))
    both = lax.dot_general(forward, trace, dims, precision=HIGH, preferred_element_type=F32)
    half = both.shape[0] // 2
    return jnp.concatenate([both[:half], both[half:]], axis=1)


def from_spec(packed, inverse):
    half = packed.shape[1] // 2
    stacked = jnp.concatenate([packed[:, :half], packed[:, half:]], axis=0)
    dims = (((0,), (0,)), ((), ()))
    return lax.dot_general(stacked, inverse, dims, precision=HIGH, preferred_element_type=F32)


def spectra_body(forward_hbm, traces_hbm, out, forward, traces, buf, arrived):
    width = traces.shape[1]
    half = width // 2
    fetches = [pltpu.make_async_copy(forward_hbm, forward, arrived.at[2])]
    for i in range(2):
        part = pl.ds(i * half, half)
        fetches.append(
            pltpu.make_async_copy(traces_hbm.at[:, part], traces.at[:, part], arrived.at[i])
        )
    for fetch in fetches:
        fetch.start()
    fetches[0].wait()
    for n in range(width):
        if n % half == 0:
            fetches[1 + n // half].wait()
        buf[:, n, :] = to_spec(forward[...], traces[:, n, :])
    out[...] = buf[...].astype(BF16)


def spectra(forward, traces):
    count, lanes = forward.shape[0] // 2, 2 * traces.shape[0]
    shape = (count, traces.shape[1], lanes)
    hbm = pltpu.HBM
    return pl.pallas_call(
        spectra_body,
        in_specs=[pl.BlockSpec(memory_space=hbm)] * 2,
        out_specs=pl.BlockSpec(memory_space=pltpu.VMEM),
        out_shape=pltpu.VMEM(shape, BF16),
        scratch_shapes=[
            pltpu.VMEM(forward.shape, F32),
            pltpu.VMEM(traces.shape, F32),
            pltpu.VMEM(shape, F32),
            pltpu.SemaphoreType.DMA((3,)),
        ],
        compiler_params=pltpu.CompilerParams(vmem_limit_bytes=4 << 20),
        name="spectra",
    )(*[pltpu.with_memory_space_constraint(arg, hbm) for arg in (forward, traces)])


def middle_body(forward, inverse, onset, plus, minus, share, far, upgoing, out, total, buf):
    ring = plus[...].astype(F32) + minus[...].astype(F32)
    total[...] = ring + (share[...] + far[1].astype(F32))
    points, width, samples = upgoing.shape
    time = lax.broadcasted_iota(jnp.int32, (points, samples), 1)
    for n in range(width):
        trace = from_spec(total[:, n, :], inverse[...])
        trace = jnp.where(time < onset[:, n : n + 1], trace, 0.0)
        upgoing[:, n, :] = trace
        buf[:, n, :] = to_spec(forward[...], trace)
    out[...] = buf[...].astype(BF16)


def last_body(inverse, onset, first, kept, taken, out_hbm, downgoing, total, sent):
    total[...] = kept[...] + taken[...].astype(F32)
    points, width, samples = downgoing.shape
    half = width // 2
    time = lax.broadcasted_iota(jnp.int32, (points, samples), 1)
    stores = []
    for n in range(width):
        trace = from_spec(total[:, n, :], inverse[...])
        trace = jnp.where(time < onset[:, n : n + 1], trace, 0.0)
        downgoing[:, n, :] = first[:, n, :] - trace
        if n % half == half - 1:
            part = pl.ds(n + 1 - half, half)
            stores.append(
                pltpu.make_async_copy(
                    downgoing.at[:, part], out_hbm.at[:, part], sent.at[n // half]
                )
            )
            stores[-1].start()
    for store in stores:
        store.wait()


def last(*args):
    vmem = pl.BlockSpec(memory_space=pltpu.VMEM)
    shape, spectrum = args[2].shape, args[3].shape
    return pl.pallas_call(
        last_body,
        in_specs=[vmem] * len(args),
        out_specs=pl.BlockSpec(memory_space=pltpu.HBM),
        out_shape=pltpu.HBM(shape, F32),
        scratch_shapes=[
            pltpu.VMEM(shape, F32),
            pltpu.VMEM(spectrum, F32),
            pltpu.SemaphoreType.DMA((2,)),
        ],
        compiler_params=pltpu.CompilerParams(vmem_limit_bytes=4 << 20),
        name="last",
    )(*[pltpu.with_memory_space_constraint(arg, pltpu.VMEM) for arg in args])


def cross(direct, turned, sign):
    half = turned.shape[1] // 2
    lane = lax.broadcasted_iota(jnp.int32, turned.shape, 1)
    swapped = pltpu.roll(turned, half, 1)
    return direct + jnp.where(lane < half, -sign * swapped, sign * swapped)


def stream(kernel, held_kernel, arrived, row, prepare, one):
    groups = kernel.shape[1] // UNROLL
    rows = pl.ds(row, held_kernel.shape[2])

    def fetch(i):
        part = pl.ds(i * UNROLL, UNROLL)
        return pltpu.make_async_copy(
            kernel.at[:, part, rows], held_kernel.at[:, part], arrived.at[i]
        )

    for i in range(groups):
        fetch(i).start()
    prepare()

    def step(i, carry):
        fetch(i).wait()
        for u in range(UNROLL):
            one(i * UNROLL + u, u)
        return carry

    lax.fori_loop(0, groups, step, 0)


def pack_body(*refs):
    for i, ref in enumerate(refs[:-1]):
        refs[-1][i] = ref[...]


def unpack(refs, spec, places):
    places = list(places)
    for ref in refs:
        if len(ref.shape) == 3:
            spec[:, places.pop(0)] = ref[...]
        else:
            for i in range(ref.shape[0]):
                spec[:, places.pop(0)] = ref[i]


def conv_body(source, *refs, spots, pieces, dyh, slots):
    ins, outs, (spec, kernel, arrived) = refs[:pieces], refs[pieces:-3], refs[-3:]
    width, lanes = ins[0].shape[-2:]
    size = NZ * width
    z = lax.axis_index("z")
    firsts = [pl.multiple_of(((z + dz) & (NZ - 1)) * width, width) for dz in range(NZ)]
    row = pl.multiple_of(((lax.axis_index("yh") + dyh) & 1) * size, size)

    def prepare():
        unpack(ins, spec, [src_at(*spot) for spot in spots])

    def one(kk, u):
        rhs = spec[kk].reshape(len(spots) * width, lanes)
        rows = [kernel[c, kk, pl.ds(first, width), :] for c in range(2) for first in firsts]
        both = jnp.dot(jnp.concatenate(rows, axis=0), rhs, preferred_element_type=F32)
        out = cross(both[:size], both[size:], 1.0)
        for ref, slot in zip(outs, slots):
            for i, dz in enumerate(slot):
                part = out[dz * width : (dz + 1) * width].astype(ref.dtype)
                if len(slot) > 1:
                    ref[i, kk] = part
                else:
                    ref[kk] = part

    stream(source, kernel, arrived, row, prepare, one)


def corr_body(source, *refs, spots, pieces):
    ins, (away, stay, spec, total, kernel, arrived) = refs[:pieces], refs[pieces:]
    width, lanes = ins[0].shape[-2:]
    near = [src_at(a, b, 0) for a, b in PAIRS]
    far = [src_at(a, b, 1) for a, b in PAIRS]

    def prepare():
        unpack(ins, spec, [rec_at(*spot) for spot in spots])

    def one(kk, u):
        turned = spec[kk].reshape(len(spots) * width, lanes).T
        real, imag = [jnp.dot(turned, kernel[c, kk], preferred_element_type=F32) for c in range(2)]
        half = lanes // 2
        out = jnp.concatenate([real[:half] + imag[half:], real[half:] - imag[:half]], axis=0).T
        total[u] = out.reshape(-1, width, lanes)
        for j in range(len(PAIRS)):
            stay[j, kk] = total[u, near[j]]
            away[j, kk] = total[u, far[j]].astype(BF16)

    stream(source, kernel, arrived, 0, prepare, one)


def join_body(share, far, out):
    out[...] = (share[...] + far[...].astype(F32)).astype(BF16)


def hop_body(taken, share, far, out, *, at):
    out[...] = (taken[...].astype(F32) + share[...] + far[at].astype(F32)).astype(BF16)


def held(stay, taken, s, b):
    j = PAIRS.index((1 - s, b))
    return stay[j] + taken[j].astype(F32)


def lead_x_body(stay, taken, out_p, out_m):
    out_p[...] = held(stay, taken, 0, 2).astype(BF16)
    out_m[...] = held(stay, taken, 1, 2).astype(BF16)


def turn_x_body(plus, minus, stay, taken, out_p, out_m):
    out_p[0] = (plus[...].astype(F32) + held(stay, taken, 0, 1)).astype(BF16)
    out_p[1] = held(stay, taken, 1, 1).astype(BF16)
    out_m[0] = held(stay, taken, 0, 3).astype(BF16)
    out_m[1] = (minus[...].astype(F32) + held(stay, taken, 1, 3)).astype(BF16)


def meet_x_body(plus, minus, stay, taken, send, keep):
    send[...] = (plus[0].astype(F32) + minus[0].astype(F32) + held(stay, taken, 0, 0)).astype(BF16)
    keep[...] = plus[1].astype(F32) + minus[1].astype(F32) + held(stay, taken, 1, 0)


def move(value, axis, step):
    size = lax.axis_size(axis)
    return lax.ppermute(value, axis, [(i, (i + step) % size) for i in range(size)])


def per_device(kernel, focusing, first_arrival, onset):
    points, width, samples = focusing.shape
    count = kernel.shape[1]
    lanes = 2 * points
    forward = jnp.asarray(table(count, samples, False))
    inverse = forward * (2.0 / samples)
    rinverse = jnp.asarray(table(count, samples, True)) * (2.0 / samples)
    src, rec = src_at(0, 0, 0), rec_at(0, 0)
    one, two = (count, width, lanes), (2, count, width, lanes)
    limits_up = lax.dynamic_slice_in_dim(onset, (src * 2 * NZ + rec) * width, width, 1)
    limits_down = lax.dynamic_slice_in_dim(onset, (rec * 4 * NX + src) * width, width, 1)
    buf = pltpu.VMEM(one, F32)
    arrived = pltpu.SemaphoreType.DMA((count // UNROLL,))
    half_kernel = (2, count, kernel.shape[2] // 2, kernel.shape[3])

    own = spectra(forward, focusing)
    near = {(0, 0): own}
    near[0, -1] = move(own, "x", 1)
    near[0, 1] = move(own, "x", -1)
    near[1, 0] = move(own, "yl", 1)
    near[0, 2] = move(near[0, -1], "x", 1)
    near[1, 1] = move(near[1, 0], "x", -1)
    near[1, -1] = move(near[1, 0], "x", 1)
    near[1, 2] = move(near[1, 1], "x", -1)
    groups = [[(0, 0), (1, 0), (0, -1), (0, 1)], [(1, 1), (1, -1), (0, 2), (1, 2)]]
    pieces = list(near.values())
    spots = [key + (0,) for key in near] + [key + (1,) for group in groups for key in group]
    for group in groups:
        (packed,) = local(pack_body, [((len(group),) + one, BF16)], [near[key] for key in group])
        pieces.append(move(packed, "c", 1))
    full = (len(spots), width, lanes)

    def conv(dyh, slots, dtype):
        return local(
            functools.partial(
                conv_body, spots=spots, pieces=len(pieces), dyh=dyh, slots=slots
            ),
            [(((len(slot),) if len(slot) > 1 else ()) + one, dtype) for slot in slots],
            pieces,
            [pltpu.VMEM((count,) + full, BF16), pltpu.VMEM(half_kernel, BF16), arrived],
            9,
            kernel,
        )

    slots = [(4,), (5,), (3, 6), (2, 7), (1, 0)]
    far = [move(value, "yh", 1) for value in conv(1, slots, BF16)]
    share = conv(0, [(dz,) for dz in range(NZ)], F32)
    (plus,) = local(join_body, [(one, BF16)], [share[4], far[0]])
    plus = move(plus, "z", 1)
    (minus,) = local(join_body, [(one, BF16)], [share[5], far[1]])
    minus = move(minus, "z", -1)
    for dz, group, at in ((3, 2, 0), (2, 3, 0), (1, 4, 0)):
        body = functools.partial(hop_body, at=at)
        (plus,) = local(body, [(one, BF16)], [plus, share[dz], far[group]])
        plus = move(plus, "z", 1)
    for dz, group, at in ((6, 2, 1), (7, 3, 1)):
        body = functools.partial(hop_body, at=at)
        (minus,) = local(body, [(one, BF16)], [minus, share[dz], far[group]])
        minus = move(minus, "z", -1)
    upgoing, mine = local(
        middle_body,
        [(focusing.shape, F32), (one, BF16)],
        [forward, inverse, limits_up, plus, minus, share[0], far[4]],
        [buf, buf],
    )

    pieces, spots = [mine, move(mine, "yh", 1)], [(0, 0), (1, 0)]
    plus = minus = mine
    for i in range(1, NZ // 2):
        plus, minus = move(plus, "z", 1), move(minus, "z", -1)
        (pair,) = local(pack_body, [(two, BF16)], [plus, minus])
        pieces += [plus, minus, move(pair, "yh", 1)]
        spots += [(s, dz) for s in range(2) for dz in (-i, i)]
    plus = move(plus, "z", 1)
    pieces += [plus, move(plus, "yh", 1)]
    spots += [(s, NZ // 2) for s in range(2)]
    away, stay = local(
        functools.partial(corr_body, spots=spots, pieces=len(pieces)),
        [((len(PAIRS),) + one, BF16), ((len(PAIRS),) + one, F32)],
        pieces,
        [pltpu.VMEM((count,) + full, BF16), pltpu.VMEM((UNROLL,) + full, F32)]
        + [pltpu.VMEM(kernel.shape, BF16), arrived],
        18,
        kernel,
    )
    taken = move(away, "c", 1)
    plus, minus = local(lead_x_body, [(one, BF16)] * 2, [stay, taken])
    plus, minus = move(plus, "x", 1), move(minus, "x", -1)
    plus, minus = local(turn_x_body, [(two, BF16)] * 2, [plus, minus, stay, taken])
    plus, minus = move(plus, "x", 1), move(minus, "x", -1)
    send, keep = local(meet_x_body, [(one, BF16), (one, F32)], [plus, minus, stay, taken])
    taken = move(send, "yl", 1)
    downgoing = last(rinverse, limits_down, first_arrival, keep, taken)
    return upgoing, downgoing


def solution(mesh):
    fine = Mesh(mesh.devices.reshape(2, NX, 2, 2, NZ), ("yl", "x", "c", "yh", "z"))
    src, rec = ("yl", "x", "c"), ("yh", "z")
    in_specs = (P(None, None, src, rec), P(None, rec + src, None), P(None, rec + src, None), P())
    out_specs = (P(None, src + rec, None), P(None, rec + src, None))

    return jax.shard_map(
        per_device, mesh=fine, in_specs=in_specs, out_specs=out_specs, check_vma=False
    )
```
